256 devices in a mesh: row: 16 (over x, y_hi, core), col: 8 (over z), depth: 2 (over y_lo).
Axes of the slice: x: 4, y: 4 (y_hi: 2, y_lo: 2; y = y_hi * 2 + y_lo), z: 8, core: 2. Of those that a mesh axis runs over, the one named last changes fastest.
Arguments:
- front_matrix: float32 [2, 8192, 8192], P('depth', 'row', 'col'), as said below
- block_mask: int32 [2, 64, 64], P('depth', 'row', 'col'), may hold values 0 or 1
- supernode_width: int32 [2, 3], P('depth'), may hold values from 128 to 256, as said below
Outputs:
- schur: float32 [2, 8192, 8192], P('depth', 'row', 'col')
- ancestor: float32 [4096, 4096], P('row', ('col', 'depth'))
The draws below stay inside these ranges and needn't reach their ends.
Inputs may be any that keep to these rules, and one draw needn't show every extreme that they name: `front_matrix`: restricted to its first 768 rows and columns, each front is row diagonally dominant: each diagonal entry is positive and at least 1.5 times the sum of the magnitudes of the other entries of its row among those columns. `supernode_width`: each entry is a multiple of 128; in each front one supernode has the full width 256.
All inputs are finite; a program needn't handle non-finite values. No bound on the sum of `block_mask` on one device may be relied on, other than what follows from the above.
Results may differ from the reference program's by a relative error of at most 0.0001.
Values sent between devices are 32-bit elements; how exact they have to be, the bound alone decides.
No kernel may reach another device: no remote copies, remote signals or barrier semaphores. Data moves between devices by JAX's collectives and lax.ppermute only.
A program may use at most 64 MiB of HBM per device.

```python
import jax
import jax.numpy as jnp
from jax import lax

F = 8192
SN = 256
BLK = 128
NSN = 3
LAYERS = 2
PIV = 768


def draw_front_matrix(key, part):
    shape_all = (LAYERS, F, F)
    key_noise = jax.random.fold_in(key, 101)
    key_across = jax.random.fold_in(key, 202)
    key_down = jax.random.fold_in(key, 303)
    noise = jax.random.normal(key_noise, shape_all, jnp.float32)
    across = jax.random.normal(key_across, (LAYERS, 1, F), jnp.float32)
    down = jax.random.normal(key_down, (LAYERS, F, 1), jnp.float32)
    position = jnp.arange(F)
    in_pivot = position < PIV
    both_pivot = (in_pivot[:, None] & in_pivot[None, :])[None]
    band_part = (in_pivot[:, None] & ~in_pivot[None, :])[None]
    panel_part = (~in_pivot[:, None] & in_pivot[None, :])[None]
    coupled = jnp.abs(noise) + 0.5 * noise
    values = jnp.where(both_pivot, coupled, noise)
    values = jnp.where(band_part, 2.0 * (across + noise), values)
    values = jnp.where(panel_part, 2.0 * (down + noise), values)
    diagonal_pos = (position[:, None] == position[None, :])[None]
    offsum = jnp.sum(jnp.where(both_pivot & ~diagonal_pos, jnp.abs(values), 0.0), axis=-1)
    diagonal = 1.5 * offsum + 1.0
    values = jnp.where(diagonal_pos & both_pivot, diagonal[:, :, None], values)
    return values.astype(jnp.float32)


def draw_supernode_width(key, part):
    key_count = jax.random.fold_in(key, 11)
    key_full = jax.random.fold_in(key, 23)
    most = SN // BLK
    counts = jax.random.randint(key_count, (LAYERS, NSN), 1, most + 1)
    full_slot = jax.random.randint(key_full, (LAYERS,), 0, NSN)
    counts = jnp.where(jnp.arange(NSN)[None, :] == full_slot[:, None], most, counts)
    return (counts * BLK).astype(jnp.int32)


def plant(array, own_key, low, top_value):
    spot = [jax.random.randint(jax.random.fold_in(own_key, axis), (), 0, length) for axis, length in enumerate(array.shape)]
    main_axis = array.shape.index(max(array.shape))
    beside = spot[:main_axis] + [(spot[main_axis] + 1) % array.shape[main_axis]] + spot[main_axis + 1:]
    return array.at[tuple(spot)].set(low).at[tuple(beside)].set(top_value)


def setup_inputs(seed: int = 0) -> dict:
    key_list = jax.random.split(jax.random.key(seed), 4)
    return {
        "front_matrix": draw_front_matrix(jax.random.fold_in(key_list[3], 71), 0),
        "block_mask": plant((jax.random.randint(key_list[1], (LAYERS, F // BLK, F // BLK), 0, 2) < 1).astype(jnp.int32), jax.random.fold_in(key_list[1], 1), 0, 1),
        "supernode_width": draw_supernode_width(jax.random.fold_in(key_list[3], 71), 0),
    }


def eliminate(matrix, widths):
    order = matrix.shape[0]
    position = jnp.arange(order)
    finished = jnp.zeros((order,), jnp.float32)
    for supernode in range(NSN):
        pivot_start = supernode * SN
        pivots = (jnp.arange(SN) < widths[supernode]).astype(jnp.float32)
        column_panel = matrix[:, pivot_start:pivot_start + SN] * pivots[None, :]
        row_band = matrix[pivot_start:pivot_start + SN, :] * pivots[:, None]
        pivot_block = matrix[pivot_start:pivot_start + SN, pivot_start:pivot_start + SN] * pivots[:, None] * pivots[None, :] + jnp.diag(1.0 - pivots)
        solved = jnp.linalg.solve(pivot_block, row_band)
        update = jnp.dot(column_panel, solved, precision=lax.Precision.HIGHEST)
        chosen = ((position >= pivot_start) & (position < pivot_start + widths[supernode])).astype(jnp.float32)
        live_set = 1.0 - finished - chosen
        matrix = matrix - live_set[:, None] * live_set[None, :] * update
        finished = finished + chosen
    return matrix

def reference(front_matrix, block_mask, supernode_width):
    blocks_per = F // BLK
    block_ids = jnp.arange(blocks_per)
    outputs = []
    ancestor = None
    for layer_index in range(LAYERS):
        kept_blocks = ((block_mask[layer_index] != 0) | (block_ids[:, None] == block_ids[None, :])).astype(jnp.float32)
        matrix = (front_matrix[layer_index].reshape(blocks_per, BLK, blocks_per, BLK) * kept_blocks[:, None, :, None]).reshape(F, F)
        matrix = eliminate(matrix, supernode_width[layer_index])
        outputs.append(matrix)
        quarter = matrix.reshape(blocks_per, BLK, blocks_per, BLK)[1::2, :, 1::2, :].reshape(F // 2, F // 2)
        if layer_index == 0:
            ancestor = quarter
        else:
            ancestor = ancestor + quarter
    return (jnp.stack(outputs), ancestor)
```

```python
import jax
import jax.numpy as jnp
from jax import lax
from jax.experimental import pallas as pl
from jax.experimental.pallas import tpu as pltpu
from jax.sharding import PartitionSpec as P

SN = 256
BLK = 128
NSN = 3
PIV = SN * NSN
ROWS = 16
COLS = 8
CHIPS = 8
XS = 4


def split(a):
    high = a.astype(jnp.bfloat16)
    low = (a - high.astype(jnp.float32)).astype(jnp.bfloat16)
    return high, low


def mul(a, b):
    return jnp.dot(a, b, preferred_element_type=jnp.float32)


def dot3(a, b):
    ah, al = a if isinstance(a, tuple) else split(a)
    bh, bl = b if isinstance(b, tuple) else split(b)
    return mul(ah, bh) + (mul(ah, bl) + mul(al, bh))


def inverse(block):
    shape = block.shape
    eye = lax.broadcasted_iota(jnp.int32, shape, 0) == lax.broadcasted_iota(jnp.int32, shape, 1)
    diagonal = jnp.where(eye, block, 0.0)
    by_row = 1.0 / jnp.sum(diagonal, axis=1, keepdims=True)
    by_col = 1.0 / jnp.sum(diagonal, axis=0, keepdims=True)
    power = jnp.where(eye, 0.0, -block * by_row)
    total = jnp.where(eye, 1.0, power)
    for step in range(5):
        parts = split(power)
        power = dot3(parts, parts)
        total = total + dot3(total, power)
    return total * by_col


def factor_kernel(info, own, other, out, matrix):
    x, core = info[0], info[1]
    for k in range(XS):
        place = lax.rem(x + k, XS) * 96
        matrix[pl.ds(pl.multiple_of(384 * core + place, 96), 96), :] = own[96 * k:96 * k + 96, :]
        matrix[pl.ds(pl.multiple_of(384 * (1 - core) + place, 96), 96), :] = other[96 * k:96 * k + 96, :]
    row_ids = lax.broadcasted_iota(jnp.int32, (SN, SN), 0)
    col_ids = lax.broadcasted_iota(jnp.int32, (SN, SN), 1)

    def block(i, j):
        keep = (row_ids < info[4 + i]) & (col_ids < info[4 + j])
        return jnp.where(keep, matrix[SN * i:SN * i + SN, SN * j:SN * j + SN], 0.0)

    def pivot(value, i):
        return jnp.where((row_ids == col_ids) & (row_ids >= info[4 + i]), 1.0, value)

    i0 = inverse(pivot(block(0, 0), 0))
    i0s = split(i0)
    v01 = split(dot3(i0s, block(0, 1)))
    v02 = split(dot3(i0s, block(0, 2)))
    m10 = split(block(1, 0))
    m20 = split(block(2, 0))
    i1 = inverse(pivot(block(1, 1) - dot3(m10, v01), 1))
    m12 = block(1, 2) - dot3(m10, v02)
    m21 = split(block(2, 1) - dot3(m20, v01))
    v12 = split(dot3(i1, m12))
    i2 = inverse(pivot(block(2, 2) - dot3(m20, v02) - dot3(m21, v12), 2))
    for n, value in enumerate((i0s, split(i1), split(i2), m10, m20, m21, v01, v02, v12)):
        out[2 * n] = value[0]
        out[2 * n + 1] = value[1]


def update_kernel(info, front, own, other, strips, blocks, *rest, per_call):
    out, quarter, left, panel, band = rest[-5:]
    step = pl.program_id(0)

    def got(n):
        return blocks[2 * n], blocks[2 * n + 1]

    def panels(offset, length, axis, shape):
        ids = offset + lax.broadcasted_iota(jnp.int32, shape, axis)
        order = jnp.full(shape, NSN, jnp.int32)
        for s in range(NSN):
            order = jnp.where((ids >= SN * s) & (ids < SN * s + info[4 + s]), s, order)
        return order

    @pl.when(step == 0)
    def _():
        z = info[2]
        for k in range(COLS):
            place = lax.rem(z + k, COLS) * 64
            panel[pl.ds(pl.multiple_of(place, 64), 64), :] = strips[64 * k:64 * k + 64, :]
        keep = lax.broadcasted_iota(jnp.int32, (512, SN), 1)
        order = panels(info[3] * 512, 512, 0, (512, 1))
        c = [jnp.where(keep < info[4 + s], panel[:, SN * s:SN * s + SN], 0.0) for s in range(NSN)]
        l0 = split(c[0])
        l1 = split(c[1] - dot3(l0, got(6)))
        l2 = split(c[2] - dot3(l0, got(7)) - dot3(l1, got(8)))
        for s, value in enumerate((l0, l1, l2)):
            live = order > s
            for part in range(2):
                left[part, :, SN * s:SN * s + SN] = jnp.where(live, value[part], jnp.zeros_like(value[part]))

    x, core = info[0], info[1]
    for k in range(XS):
        place = lax.rem(x + k, XS) * 96
        band[pl.ds(pl.multiple_of(384 * core + place, 96), 96), :] = own[96 * k:96 * k + 96, :]
        band[pl.ds(pl.multiple_of(384 * (1 - core) + place, 96), 96), :] = other[96 * k:96 * k + 96, :]
    width = band.shape[1]
    keep = lax.broadcasted_iota(jnp.int32, (SN, width), 0)
    r = [jnp.where(keep < info[4 + s], band[SN * s:SN * s + SN, :], 0.0) for s in range(NSN)]
    s0 = split(dot3(got(0), r[0]))
    s1 = split(dot3(got(1), r[1] - dot3(got(3), s0)))
    s2 = split(dot3(got(2), r[2] - dot3(got(4), s0) - dot3(got(5), s1)))
    half = info[8] if per_call else info[7]
    first = info[2] * 1024 + half * 512 + step * width
    order = panels(first, width, 1, (1, width))
    total = None
    for s, value in enumerate((s0, s1, s2)):
        live = order > s
        bh, bl = (jnp.where(live, part, jnp.zeros_like(part)) for part in value)
        ah = left[0, :, SN * s:SN * s + SN]
        al = left[1, :, SN * s:SN * s + SN]
        term = mul(ah, bh) + (mul(ah, bl) + mul(al, bh))
        total = term if total is None else total + term
    result = front[...] - total
    out[...] = result
    for i in range(2):
        for j in range(width // 256):
            quarter[128 * i:128 * i + 128, 128 * j:128 * j + 128] = result[
                256 * i + 128:256 * i + 256, 256 * j + 128:256 * j + 256
            ]


def ring(axis_size, pairs):
    return [(i, pairs(i)) for i in range(axis_size)]


def send(value, axis, pairs):
    return lax.ppermute(value, axis, pairs)


def gather_plane(piece, odd):
    height = piece.shape[0]
    mate = send(piece, "row", ring(ROWS, lambda i: i ^ 2))
    pair = jnp.concatenate([jnp.where(odd, mate, piece), jnp.where(odd, piece, mate)])
    before = send(pair, "row", ring(ROWS, lambda i: (i + 4) % ROWS))
    after = send(pair, "row", ring(ROWS, lambda i: (i - 4) % ROWS))
    far_even = send(before[:height], "row", ring(ROWS, lambda i: (i + 4) % ROWS))
    far_odd = send(after[height:], "row", ring(ROWS, lambda i: (i - 4) % ROWS))
    own = jnp.concatenate([pair, after, far_even, far_odd, before])
    other = send(own, "row", ring(ROWS, lambda i: i ^ 1))
    return own, other


def gather_line(piece):
    half = piece.shape[0] // 2
    up, down = ring(COLS, lambda i: (i + 1) % COLS), ring(COLS, lambda i: (i - 1) % COLS)
    before, after = [piece], [piece]
    for _ in range(3):
        before.append(send(before[-1], "col", up))
        after.append(send(after[-1], "col", down))
    far_high = send(before[3][:half], "col", up)
    far_low = send(after[3][half:], "col", down)
    return jnp.concatenate(after[:4] + [far_high, far_low] + before[3:0:-1])


def local(front_matrix, block_mask, supernode_width):
    row_index = lax.axis_index("row")
    col_index = lax.axis_index("col")
    depth_index = lax.axis_index("depth")
    block_rows = row_index * 4 + jnp.arange(4)
    block_cols = col_index * 8 + jnp.arange(8)
    kept = ((block_mask[0] != 0) | (block_rows[:, None] == block_cols[None, :])).astype(jnp.float32)
    matrix = (front_matrix[0].reshape(4, BLK, 8, BLK) * kept[:, None, :, None]).reshape(512, 1024)
    core = row_index % 2
    info = jnp.concatenate([
        jnp.stack([row_index // 4, core, col_index, row_index]).astype(jnp.int32),
        supernode_width[0],
        jnp.stack([1 - depth_index, depth_index]).astype(jnp.int32),
    ])

    panels = exchange(matrix, row_index, col_index)
    return compute(info, matrix, *panels)


def exchange(matrix, row_index, col_index):
    odd = (row_index // 2) % 2 == 1
    moved = send(matrix[384:512], "row", [(0, 1)])
    source = jnp.where(row_index == 1, jnp.concatenate([moved, matrix[:256]]), matrix[:384])
    parts = [send(source[48 * q:48 * q + 48], "row", [(0, 2 * q), (1, 2 * q + 1)]) for q in range(1, CHIPS)]
    piece = jnp.where(row_index < 2, source[:48], sum(parts[1:], parts[0]))

    panel = matrix[:, :PIV]
    parts = [send(panel[64 * z:64 * z + 64], "col", [(0, z)]) for z in range(1, COLS)]
    strip = jnp.where(col_index == 0, panel[:64], sum(parts[1:], parts[0]))

    core_piece = piece[:, :PIV]
    parts = [send(core_piece, "col", [(0, z)]) for z in range(1, COLS)]
    pivot_piece = jnp.where(col_index == 0, core_piece, sum(parts[1:], parts[0]))

    band_own, band_other = gather_plane(piece, odd)
    pivot_own, pivot_other = gather_plane(pivot_piece, odd)
    strips = gather_line(strip)
    return band_own, band_other, pivot_own, pivot_other, strips


def compute(info, matrix, band_own, band_other, pivot_own, pivot_other, strips):
    blocks = pl.pallas_call(
        factor_kernel,
        grid_spec=pltpu.PrefetchScalarGridSpec(
            num_scalar_prefetch=1,
            grid=(),
            in_specs=[pl.BlockSpec(memory_space=pltpu.VMEM)] * 2,
            out_specs=pl.BlockSpec(memory_space=pltpu.VMEM),
            scratch_shapes=[pltpu.VMEM((PIV, PIV), jnp.float32)],
        ),
        out_shape=jax.ShapeDtypeStruct((18, SN, SN), jnp.bfloat16),
        name="factor",
    )(info, pivot_own, pivot_other)

    width = 256

    def update(which, previous):
        def at(j, info):
            return (0, info[7 + which] * 2 + j)

        whole = lambda shape: pl.BlockSpec(shape, lambda j, info: (0,) * len(shape))
        extra = [] if previous is None else [previous]
        return pl.pallas_call(
            lambda *refs: update_kernel(*refs, per_call=which),
            grid_spec=pltpu.PrefetchScalarGridSpec(
                num_scalar_prefetch=1,
                grid=(2,),
                in_specs=[
                    pl.BlockSpec((512, width), at),
                    pl.BlockSpec((384, width), at),
                    pl.BlockSpec((384, width), at),
                    whole((512, PIV)),
                    whole((18, SN, SN)),
                ] + [pl.BlockSpec(memory_space=pl.ANY)] * len(extra),
                out_specs=[pl.BlockSpec((512, width), at), pl.BlockSpec((256, width // 2), lambda j, info: (0, j))],
                scratch_shapes=[
                    pltpu.VMEM((2, 512, PIV), jnp.bfloat16),
                    pltpu.VMEM((512, PIV), jnp.float32),
                    pltpu.VMEM((PIV, width), jnp.float32),
                ],
            ),
            out_shape=[
                jax.ShapeDtypeStruct((512, 1024), jnp.float32),
                jax.ShapeDtypeStruct((256, 256), jnp.float32),
            ],
            input_output_aliases={} if previous is None else {6: 0},
            name="update",
        )(info, matrix, band_own, band_other, strips, blocks, *extra)

    partial, leaving = update(0, None)
    arriving = send(leaving, "depth", [(0, 1), (1, 0)])
    result, staying = update(1, partial)
    return result[None], staying + arriving


def solution(mesh):
    placed = (P("depth", "row", "col"), P("depth", "row", "col"), P("depth", None))
    return jax.shard_map(
        local,
        mesh=mesh,
        in_specs=placed,
        out_specs=(P("depth", "row", "col"), P("row", ("col", "depth"))),
        check_vma=False,
    )
```

```python
import jax
import jax.numpy as jnp
from jax import lax
from jax.experimental import pallas as pl
from jax.experimental.pallas import tpu as pltpu
from jax.sharding import PartitionSpec as P


SN = 256
BLK = 128
NSN = 3
PIV = SN * NSN
ROWS = 16
COLS = 8
CHIPS = 8
XS = 4


def split(a):
    high = a.astype(jnp.bfloat16)
    low = (a - high.astype(jnp.float32)).astype(jnp.bfloat16)
    return high, low


def mul(a, b):
    return jnp.dot(a, b, preferred_element_type=jnp.float32)


def dot3(a, b):
    ah, al = a if isinstance(a, tuple) else split(a)
    bh, bl = b if isinstance(b, tuple) else split(b)
    return mul(ah, bh) + (mul(ah, bl) + mul(al, bh))


def inverse(block):
    shape = block.shape
    eye = lax.broadcasted_iota(jnp.int32, shape, 0) == lax.broadcasted_iota(jnp.int32, shape, 1)
    diagonal = jnp.where(eye, block, 0.0)
    by_row = 1.0 / jnp.sum(diagonal, axis=1, keepdims=True)
    by_col = 1.0 / jnp.sum(diagonal, axis=0, keepdims=True)
    power = jnp.where(eye, 0.0, -block * by_row)
    total = jnp.where(eye, 1.0, power)
    for _ in range(5):
        parts = split(power)
        power = dot3(parts, parts)
        total = total + dot3(total, power)
    return total * by_col


def place_rows(target, own, other, info):
    x, core = info[0], info[1]
    for parts, c in ((own, core), (other, 1 - core)):
        for k in range(XS):
            for e in range(2):
                chip = 2 * lax.rem(x + k, XS) + e
                target[pl.ds(pl.multiple_of(512 * c + 32 * chip, 32), 32), :] = parts[k][48 * e:48 * e + 32, :]
                target[pl.ds(pl.multiple_of(256 + 128 * c + 16 * chip, 16), 16), :] = parts[k][48 * e + 32:48 * e + 48, :]


def pieces_kernel(info, matrix, moved, *out):
    first = info[1] == 0
    for q in range(CHIPS):
        out[q][:32, :] = matrix[32 * q:32 * q + 32, :]
        mine = matrix[256 + 16 * q:272 + 16 * q, :]
        out[q][32:, :] = jnp.where(first, mine, moved[16 * q:16 * q + 16, :])


def factor_kernel(info, *refs):
    out, matrix = refs[8:]
    place_rows(matrix, refs[:4], refs[4:8], info)
    row_ids = lax.broadcasted_iota(jnp.int32, (SN, SN), 0)
    col_ids = lax.broadcasted_iota(jnp.int32, (SN, SN), 1)

    def block(i, j):
        keep = (row_ids < info[4 + i]) & (col_ids < info[4 + j])
        return jnp.where(keep, matrix[SN * i:SN * i + SN, SN * j:SN * j + SN], 0.0)

    def pivot(value, i):
        return jnp.where((row_ids == col_ids) & (row_ids >= info[4 + i]), 1.0, value)

    i0 = inverse(pivot(block(0, 0), 0))
    i0s = split(i0)
    v01 = split(dot3(i0s, block(0, 1)))
    v02 = split(dot3(i0s, block(0, 2)))
    m10 = split(block(1, 0))
    m20 = split(block(2, 0))
    i1 = inverse(pivot(block(1, 1) - dot3(m10, v01), 1))
    m12 = block(1, 2) - dot3(m10, v02)
    m21 = split(block(2, 1) - dot3(m20, v01))
    v12 = split(dot3(i1, m12))
    i2 = inverse(pivot(block(2, 2) - dot3(m20, v02) - dot3(m21, v12), 2))
    for n, value in enumerate((i0s, split(i1), split(i2), m10, m20, m21, v01, v02, v12)):
        out[2 * n] = value[0]
        out[2 * n + 1] = value[1]


def order_of(info, offset, axis, shape):
    ids = offset + lax.broadcasted_iota(jnp.int32, shape, axis)
    order = jnp.full(shape, NSN, jnp.int32)
    for s in range(NSN):
        order = jnp.where((ids >= SN * s) & (ids < SN * s + info[4 + s]), s, order)
    return order


def left_of(info, strips, got, left, panel):
    z = info[2]
    for k in range(COLS):
        place = lax.rem(z + k, COLS) * 64
        if k == 4:
            panel[pl.ds(pl.multiple_of(place, 64), 32), :] = strips[4][...]
            panel[pl.ds(pl.multiple_of(place + 32, 32), 32), :] = strips[5][...]
        else:
            panel[pl.ds(pl.multiple_of(place, 64), 64), :] = strips[k if k < 4 else k + 1][...]
    keep = lax.broadcasted_iota(jnp.int32, (512, SN), 1)
    order = order_of(info, info[3] * 512, 0, (512, 1))
    c = [jnp.where(keep < info[4 + s], panel[:, SN * s:SN * s + SN], 0.0) for s in range(NSN)]
    l0 = split(c[0])
    l1 = split(c[1] - dot3(l0, got(6)))
    l2 = split(c[2] - dot3(l0, got(7)) - dot3(l1, got(8)))
    for s, value in enumerate((l0, l1, l2)):
        live = order > s
        for part in range(2):
            left[part, :, SN * s:SN * s + SN] = jnp.where(live, value[part], jnp.zeros_like(value[part]))


def update_kernel(info, front, *refs, second):
    own, other, blocks = refs[:4], refs[4:8], refs[8]
    step = pl.program_id(0)

    def got(n):
        return blocks[2 * n], blocks[2 * n + 1]

    if second:
        left, _, out, quarter, band = refs[9:]
    else:
        strips, (out, quarter, left, band, panel) = refs[9:18], refs[18:]

        @pl.when(step == 0)
        def _():
            left_of(info, strips, got, left, panel)

    place_rows(band, own, other, info)
    width = band.shape[1]
    keep = lax.broadcasted_iota(jnp.int32, (SN, width), 0)
    r = [jnp.where(keep < info[4 + s], band[SN * s:SN * s + SN, :], 0.0) for s in range(NSN)]
    s0 = split(dot3(got(0), r[0]))
    s1 = split(dot3(got(1), r[1] - dot3(got(3), s0)))
    s2 = split(dot3(got(2), r[2] - dot3(got(4), s0) - dot3(got(5), s1)))
    half = info[8] if second else info[7]
    order = order_of(info, info[2] * 1024 + half * 512 + step * width, 1, (1, width))
    total = None
    for s, value in enumerate((s0, s1, s2)):
        live = order > s
        bh, bl = (jnp.where(live, part, jnp.zeros_like(part)) for part in value)
        ah = left[0, :, SN * s:SN * s + SN]
        al = left[1, :, SN * s:SN * s + SN]
        term = mul(ah, bh) + (mul(ah, bl) + mul(al, bh))
        total = term if total is None else total + term
    result = front[...] - total
    out[...] = result
    for i in range(2):
        for j in range(width // 256):
            quarter[128 * i:128 * i + 128, 128 * j:128 * j + 128] = result[
                256 * i + 128:256 * i + 256, 256 * j + 128:256 * j + 256
            ]


def each(axis_size, target):
    return [(i, target(i)) for i in range(axis_size)]


X_UP = each(ROWS, lambda i: (i + 4) % ROWS)
X_DOWN = each(ROWS, lambda i: (i - 4) % ROWS)
MATE = each(ROWS, lambda i: i ^ 2)
CORE = each(ROWS, lambda i: i ^ 1)
Z_UP = each(COLS, lambda i: (i + 1) % COLS)
Z_DOWN = each(COLS, lambda i: (i - 1) % COLS)
Z_ODD = [(z, z + 1) for z in range(0, COLS, 2)]


def gather_plane(piece, odd):
    height = piece.shape[0]
    mate = lax.ppermute(piece, "row", MATE)
    pair = jnp.concatenate([jnp.where(odd, mate, piece), jnp.where(odd, piece, mate)])
    before = lax.ppermute(pair, "row", X_UP)
    after = lax.ppermute(pair, "row", X_DOWN)
    far_even = lax.ppermute(before[:height], "row", X_UP)
    far_odd = lax.ppermute(after[height:], "row", X_DOWN)
    own = [pair, after, jnp.concatenate([far_even, far_odd]), before]
    return own, [lax.ppermute(part, "row", CORE) for part in own]


def gather_line(piece):
    half = piece.shape[0] // 2
    before, after = [piece], [piece]
    for _ in range(1, 4):
        before.append(lax.ppermute(before[-1], "col", Z_UP))
        after.append(lax.ppermute(after[-1], "col", Z_DOWN))
    far_high = lax.ppermute(before[3][:half], "col", Z_UP)
    far_low = lax.ppermute(after[3][half:], "col", Z_DOWN)
    return after[:4] + [far_high, far_low] + before[3:0:-1]


def exchange(matrix, info, row_index, col_index):
    odd = (row_index // 2) % 2 == 1
    odd_col = col_index % 2 == 1
    moved = lax.ppermute(matrix[384:512], "row", [(0, 1)])
    panel = matrix[:, :PIV]
    parts = [lax.ppermute(panel[64 * z:64 * z + 128], "col", [(0, z)]) for z in (2, 4, 6)]
    strip = jnp.where(col_index == 0, panel[:128], parts[0] + parts[1] + parts[2])
    strip = jnp.where(odd_col, lax.ppermute(strip[64:], "col", Z_ODD), strip[:64])

    pieces = pl.pallas_call(
        pieces_kernel,
        grid_spec=pltpu.PrefetchScalarGridSpec(
            num_scalar_prefetch=1,
            grid=(1,),
            in_specs=[pl.BlockSpec((384, 1024), lambda i, info: (0, 0)), pl.BlockSpec((128, 1024), lambda i, info: (0, 0))],
            out_specs=[pl.BlockSpec((48, 1024), lambda i, info: (0, 0))] * CHIPS,
        ),
        out_shape=[jax.ShapeDtypeStruct((48, 1024), jnp.float32)] * CHIPS,
        name="pieces",
    )(info, matrix, moved)
    parts = [lax.ppermute(pieces[q], "row", [(0, 2 * q), (1, 2 * q + 1)]) for q in range(1, CHIPS)]
    piece = jnp.where(row_index < 2, pieces[0], sum(parts[1:], parts[0]))

    core_piece = piece[:, :PIV]
    parts = [lax.ppermute(core_piece, "col", [(0, z)]) for z in (4, 2, 6)]
    pivot_piece = jnp.where(col_index == 0, core_piece, parts[0] + parts[1] + parts[2])
    pivot_piece = jnp.where(odd_col, lax.ppermute(pivot_piece, "col", Z_ODD), pivot_piece)

    return gather_plane(piece, odd), gather_plane(pivot_piece, odd), gather_line(strip)


def compute(info, matrix, band, pivot, strips):
    vmem = pl.BlockSpec(memory_space=pltpu.VMEM)
    blocks = pl.pallas_call(
        factor_kernel,
        grid_spec=pltpu.PrefetchScalarGridSpec(
            num_scalar_prefetch=1,
            grid=(),
            in_specs=[vmem] * 8,
            out_specs=vmem,
            scratch_shapes=[pltpu.VMEM((PIV, PIV), jnp.float32)],
        ),
        out_shape=jax.ShapeDtypeStruct((18, SN, SN), jnp.bfloat16),
        name="factor",
    )(info, *pivot[0], *pivot[1])

    width = 256

    def update(which, *inputs):
        def at(j, info):
            return (0, info[7 + which] * 2 + j)

        whole = lambda shape: pl.BlockSpec(shape, lambda j, info: (0,) * len(shape))
        left_shape = (2, 512, PIV)
        if which:
            specs = [whole(left_shape), pl.BlockSpec(memory_space=pl.ANY)]
        else:
            specs = [whole(value.shape) for value in inputs]
        return pl.pallas_call(
            lambda *refs: update_kernel(*refs, second=which == 1),
            grid_spec=pltpu.PrefetchScalarGridSpec(
                num_scalar_prefetch=1,
                grid=(2,),
                in_specs=[pl.BlockSpec((512, width), at)] + [pl.BlockSpec((96, width), at)] * 8 + [whole((18, SN, SN))] + specs,
                out_specs=[
                    pl.BlockSpec((512, width), at),
                    pl.BlockSpec((256, width // 2), lambda j, info: (0, j)),
                ] + [whole(left_shape)] * (1 - which),
                scratch_shapes=[pltpu.VMEM((PIV, width), jnp.float32)] + [pltpu.VMEM((512, PIV), jnp.float32)] * (1 - which),
            ),
            out_shape=[
                jax.ShapeDtypeStruct((512, 1024), jnp.float32),
                jax.ShapeDtypeStruct((256, 256), jnp.float32),
            ] + [jax.ShapeDtypeStruct(left_shape, jnp.bfloat16)] * (1 - which),
            input_output_aliases={12: 0} if which else {},
            name="update",
        )(info, matrix, *band[0], *band[1], blocks, *inputs)

    partial, leaving, left = update(0, *strips)
    arriving = lax.ppermute(leaving, "depth", [(0, 1), (1, 0)])
    result, staying = update(1, left, partial)
    return result[None], staying + arriving


def local(front_matrix, block_mask, supernode_width):
    row_index = lax.axis_index("row")
    col_index = lax.axis_index("col")
    depth_index = lax.axis_index("depth")
    block_rows = row_index * 4 + jnp.arange(4)
    block_cols = col_index * 8 + jnp.arange(8)
    kept = ((block_mask[0] != 0) | (block_rows[:, None] == block_cols[None, :])).astype(jnp.float32)
    kept = jnp.broadcast_to(kept[:, :, None], (4, 8, BLK)).reshape(4, 1, 1024)
    matrix = (front_matrix[0].reshape(4, BLK, 1024) * kept).reshape(512, 1024)
    info = jnp.concatenate([
        jnp.stack([row_index // 4, row_index % 2, col_index, row_index]).astype(jnp.int32),
        supernode_width[0],
        jnp.stack([1 - depth_index, depth_index]).astype(jnp.int32),
    ])
    panels = exchange(matrix, info, row_index, col_index)
    return compute(info, matrix, *panels)


def solution(mesh):
    placed = (P("depth", "row", "col"), P("depth", "row", "col"), P("depth", None))
    return jax.shard_map(
        local,
        mesh=mesh,
        in_specs=placed,
        out_specs=(P("depth", "row", "col"), P("row", ("col", "depth"))),
        check_vma=False,
    )
```

```python
import jax
import jax.numpy as jnp
from jax import lax
from jax.experimental import pallas as pl
from jax.experimental.pallas import tpu as pltpu
from jax.sharding import PartitionSpec as P


SN = 256
BLK = 128
NSN = 3
PIV = SN * NSN
ROWS = 16
COLS = 8
CHIPS = 8
XS = 4


def split(a):
    high = a.astype(jnp.bfloat16)
    low = (a - high.astype(jnp.float32)).astype(jnp.bfloat16)
    return high, low


def mul(a, b):
    return jnp.dot(a, b, preferred_element_type=jnp.float32)


def stack(a):
    return jnp.concatenate(split(a), axis=0)


def dot3(a, b):
    rows = a.shape[0] // 2
    both = mul(a, b[0])
    return both[:rows] + (both[rows:] + mul(a[:rows], b[1]))


def inverse(block):
    shape = block.shape
    eye = lax.broadcasted_iota(jnp.int32, shape, 0) == lax.broadcasted_iota(jnp.int32, shape, 1)
    diagonal = jnp.where(eye, block, 0.0)
    by_row = 1.0 / jnp.sum(diagonal, axis=1, keepdims=True)
    by_col = 1.0 / jnp.sum(diagonal, axis=0, keepdims=True)
    power = jnp.where(eye, 0.0, -block * by_row)
    total = jnp.where(eye, 1.0, power)
    for _ in range(5):
        parts = split(power)
        power = dot3(jnp.concatenate(parts, axis=0), parts)
        total = total + dot3(stack(total), split(power))
    return total * by_col


def place_rows(target, own, other, info, columns=slice(None)):
    x, core = info[0], info[1]
    for parts, c in ((own, core), (other, 1 - core)):
        for k in range(XS):
            for e in range(2):
                chip = 2 * lax.rem(x + k, XS) + e
                target[pl.ds(pl.multiple_of(512 * c + 32 * chip, 32), 32), :] = parts[k][48 * e:48 * e + 32, columns]
                target[pl.ds(pl.multiple_of(256 + 128 * c + 16 * chip, 16), 16), :] = parts[k][48 * e + 32:48 * e + 48, columns]


def pieces_kernel(info, matrix, moved, *out):
    first = info[1] == 0
    for q in range(CHIPS):
        out[q][:32, :] = matrix[32 * q:32 * q + 32, :]
        mine = matrix[256 + 16 * q:272 + 16 * q, :]
        out[q][32:, :] = jnp.where(first, mine, moved[16 * q:16 * q + 16, :])


def factor_kernel(info, *refs):
    out, matrix = refs[8:]
    place_rows(matrix, refs[:4], refs[4:8], info)
    row_ids = lax.broadcasted_iota(jnp.int32, (SN, SN), 0)
    col_ids = lax.broadcasted_iota(jnp.int32, (SN, SN), 1)

    def block(i, j):
        keep = (row_ids < info[4 + i]) & (col_ids < info[4 + j])
        return jnp.where(keep, matrix[SN * i:SN * i + SN, SN * j:SN * j + SN], 0.0)

    def pivot(value, i):
        return jnp.where((row_ids == col_ids) & (row_ids >= info[4 + i]), 1.0, value)

    i0 = stack(inverse(pivot(block(0, 0), 0)))
    v01 = split(dot3(i0, split(block(0, 1))))
    v02 = split(dot3(i0, split(block(0, 2))))
    m10 = stack(block(1, 0))
    m20 = stack(block(2, 0))
    i1 = stack(inverse(pivot(block(1, 1) - dot3(m10, v01), 1)))
    m12 = block(1, 2) - dot3(m10, v02)
    m21 = stack(block(2, 1) - dot3(m20, v01))
    v12 = split(dot3(i1, split(m12)))
    i2 = stack(inverse(pivot(block(2, 2) - dot3(m20, v02) - dot3(m21, v12), 2)))
    for n, value in enumerate((i0, i1, i2, m10, m20, m21)):
        out[n] = value
    for n, value in enumerate((v01, v02, v12)):
        out[6 + n, :SN] = value[0]
        out[6 + n, SN:] = value[1]


def order_of(info, offset, axis, shape):
    ids = offset + lax.broadcasted_iota(jnp.int32, shape, axis)
    order = jnp.full(shape, NSN, jnp.int32)
    for s in range(NSN):
        order = jnp.where((ids >= SN * s) & (ids < SN * s + info[4 + s]), s, order)
    return order


def left_of(info, strips, got, left, panel):
    z = info[2]
    for k in range(COLS):
        place = lax.rem(z + k, COLS) * 64
        if k == 4:
            panel[pl.ds(pl.multiple_of(place, 64), 32), :] = strips[4][...]
            panel[pl.ds(pl.multiple_of(place + 32, 32), 32), :] = strips[5][...]
        else:
            panel[pl.ds(pl.multiple_of(place, 64), 64), :] = strips[k if k < 4 else k + 1][...]
    keep = lax.broadcasted_iota(jnp.int32, (512, SN), 1)
    order = order_of(info, info[3] * 512, 0, (512, 1))
    c = [jnp.where(keep < info[4 + s], panel[:, SN * s:SN * s + SN], 0.0) for s in range(NSN)]
    l0 = stack(c[0])
    l1 = stack(c[1] - dot3(l0, got(6)))
    l2 = stack(c[2] - dot3(l0, got(7)) - dot3(l1, got(8)))
    live = jnp.concatenate([order, order], axis=0)
    for s, value in enumerate((l0, l1, l2)):
        left[:, SN * s:SN * s + SN] = jnp.where(live > s, value, jnp.zeros_like(value))


def update_kernel(info, front, *refs, second):
    own, other, blocks = refs[:4], refs[4:8], refs[8]
    step = pl.program_id(0)

    def got(n):
        return blocks[n, :SN], blocks[n, SN:]

    if second:
        left, _, out, quarter, band = refs[9:]
    else:
        strips, (out, quarter, left, band, panel) = refs[9:18], refs[18:]

        @pl.when(step == 0)
        def _():
            left_of(info, strips, got, left, panel)

    half = info[8] if second else info[7]
    width = band.shape[1]
    columns = pl.ds(pl.multiple_of(half * 512 + step * width, width), width)
    place_rows(band, own, other, info, columns)
    keep = lax.broadcasted_iota(jnp.int32, (SN, width), 0)
    r = [jnp.where(keep < info[4 + s], band[SN * s:SN * s + SN, :], 0.0) for s in range(NSN)]
    s0 = split(dot3(blocks[0], split(r[0])))
    s1 = split(dot3(blocks[1], split(r[1] - dot3(blocks[3], s0))))
    s2 = split(dot3(blocks[2], split(r[2] - dot3(blocks[4], s0) - dot3(blocks[5], s1))))
    order = order_of(info, info[2] * 1024 + half * 512 + step * width, 1, (1, width))
    total = None
    for s, value in enumerate((s0, s1, s2)):
        live = order > s
        masked = tuple(jnp.where(live, part, jnp.zeros_like(part)) for part in value)
        term = dot3(left[:, SN * s:SN * s + SN], masked)
        total = term if total is None else total + term
    result = front[...] - total
    out[...] = result
    for i in range(2):
        for j in range(width // 256):
            quarter[128 * i:128 * i + 128, 128 * j:128 * j + 128] = result[
                256 * i + 128:256 * i + 256, 256 * j + 128:256 * j + 256
            ]


VMEM_WHOLE = pl.BlockSpec(memory_space=pltpu.VMEM)


def each(axis_size, target):
    return [(i, target(i)) for i in range(axis_size)]


X_UP = each(ROWS, lambda i: (i + 4) % ROWS)
X_DOWN = each(ROWS, lambda i: (i - 4) % ROWS)
MATE = each(ROWS, lambda i: i ^ 2)
CORE = each(ROWS, lambda i: i ^ 1)
Z_UP = each(COLS, lambda i: (i + 1) % COLS)
Z_DOWN = each(COLS, lambda i: (i - 1) % COLS)
Z_ODD = [(z, z + 1) for z in range(0, COLS, 2)]


def gather_plane(piece, odd):
    height = piece.shape[0]
    mate = lax.ppermute(piece, "row", MATE)
    pair = jnp.concatenate([jnp.where(odd, mate, piece), jnp.where(odd, piece, mate)])
    before = lax.ppermute(pair, "row", X_UP)
    after = lax.ppermute(pair, "row", X_DOWN)
    far_even = lax.ppermute(before[:height], "row", X_UP)
    far_odd = lax.ppermute(after[height:], "row", X_DOWN)
    own = [pair, after, jnp.concatenate([far_even, far_odd]), before]
    return own, [lax.ppermute(part, "row", CORE) for part in own]


def gather_line(piece):
    half = piece.shape[0] // 2
    before, after = [piece], [piece]
    for _ in range(1, 4):
        before.append(lax.ppermute(before[-1], "col", Z_UP))
        after.append(lax.ppermute(after[-1], "col", Z_DOWN))
    far_high = lax.ppermute(before[3][:half], "col", Z_UP)
    far_low = lax.ppermute(after[3][half:], "col", Z_DOWN)
    return after[:4] + [far_high, far_low] + before[3:0:-1]


def exchange(matrix, info, row_index, col_index):
    odd = (row_index // 2) % 2 == 1
    odd_col = col_index % 2 == 1
    moved = lax.ppermute(matrix[384:512], "row", [(0, 1)])
    panel = matrix[:, :PIV]
    parts = [lax.ppermute(panel[64 * z:64 * z + 128], "col", [(0, z)]) for z in (2, 4, 6)]
    strip = jnp.where(col_index == 0, panel[:128], parts[0] + parts[1] + parts[2])
    strip = jnp.where(odd_col, lax.ppermute(strip[64:], "col", Z_ODD), strip[:64])

    pieces = pl.pallas_call(
        pieces_kernel,
        grid_spec=pltpu.PrefetchScalarGridSpec(
            num_scalar_prefetch=1,
            grid=(),
            in_specs=[VMEM_WHOLE] * 2,
            out_specs=[VMEM_WHOLE] * CHIPS,
        ),
        out_shape=[jax.ShapeDtypeStruct((48, 1024), jnp.float32)] * CHIPS,
        name="pieces",
    )(info, matrix, moved)
    parts = [lax.ppermute(pieces[q], "row", [(0, 2 * q), (1, 2 * q + 1)]) for q in range(1, CHIPS)]
    piece = jnp.where(row_index < 2, pieces[0], sum(parts[1:], parts[0]))

    core_piece = piece[:, :PIV]
    parts = [lax.ppermute(core_piece, "col", [(0, z)]) for z in (4, 2, 6)]
    pivot_piece = jnp.where(col_index == 0, core_piece, parts[0] + parts[1] + parts[2])
    pivot_piece = jnp.where(odd_col, lax.ppermute(pivot_piece, "col", Z_ODD), pivot_piece)

    return gather_plane(piece, odd), gather_plane(pivot_piece, odd), gather_line(strip)


def compute(info, matrix, band, pivot, strips):
    blocks = pl.pallas_call(
        factor_kernel,
        grid_spec=pltpu.PrefetchScalarGridSpec(
            num_scalar_prefetch=1,
            grid=(),
            in_specs=[VMEM_WHOLE] * 8,
            out_specs=VMEM_WHOLE,
            scratch_shapes=[pltpu.VMEM((PIV, PIV), jnp.float32)],
        ),
        out_shape=jax.ShapeDtypeStruct((9, 2 * SN, SN), jnp.bfloat16),
        name="factor",
    )(info, *pivot[0], *pivot[1])

    width = 256

    def update(which, *inputs):
        def at(j, info):
            return (0, info[7 + which] * 2 + j)

        left_shape = (1024, PIV)
        specs = [VMEM_WHOLE, pl.BlockSpec(memory_space=pl.ANY)] if which else [VMEM_WHOLE] * len(inputs)
        return pl.pallas_call(
            lambda *refs: update_kernel(*refs, second=which == 1),
            grid_spec=pltpu.PrefetchScalarGridSpec(
                num_scalar_prefetch=1,
                grid=(2,),
                in_specs=[pl.BlockSpec((512, width), at)] + [VMEM_WHOLE] * 9 + specs,
                out_specs=[
                    pl.BlockSpec((512, width), at),
                    pl.BlockSpec((256, width // 2), lambda j, info: (0, j)),
                ] + [VMEM_WHOLE] * (1 - which),
                scratch_shapes=[pltpu.VMEM((PIV, width), jnp.float32)] + [pltpu.VMEM((512, PIV), jnp.float32)] * (1 - which),
            ),
            out_shape=[
                jax.ShapeDtypeStruct((512, 1024), jnp.float32),
                jax.ShapeDtypeStruct((256, 256), jnp.float32),
            ] + [jax.ShapeDtypeStruct(left_shape, jnp.bfloat16)] * (1 - which),
            input_output_aliases={12: 0} if which else {},
            name="update",
        )(info, matrix, *band[0], *band[1], blocks, *inputs)

    partial, leaving, left = update(0, *strips)
    arriving = lax.ppermute(leaving, "depth", [(0, 1), (1, 0)])
    result, staying = update(1, left, partial)
    return result[None], staying + arriving


def local(front_matrix, block_mask, supernode_width):
    row_index = lax.axis_index("row")
    col_index = lax.axis_index("col")
    depth_index = lax.axis_index("depth")
    block_rows = row_index * 4 + jnp.arange(4)
    block_cols = col_index * 8 + jnp.arange(8)
    kept = ((block_mask[0] != 0) | (block_rows[:, None] == block_cols[None, :])).astype(jnp.float32)
    kept = jnp.broadcast_to(kept[:, :, None], (4, 8, BLK)).reshape(4, 1, 1024)
    matrix = (front_matrix[0].reshape(4, BLK, 1024) * kept).reshape(512, 1024)
    info = jnp.concatenate([
        jnp.stack([row_index // 4, row_index % 2, col_index, row_index]).astype(jnp.int32),
        supernode_width[0],
        jnp.stack([1 - depth_index, depth_index]).astype(jnp.int32),
    ])
    panels = exchange(matrix, info, row_index, col_index)
    return compute(info, matrix, *panels)


def solution(mesh):
    placed = (P("depth", "row", "col"), P("depth", "row", "col"), P("depth", None))
    return jax.shard_map(
        local,
        mesh=mesh,
        in_specs=placed,
        out_specs=(P("depth", "row", "col"), P("row", ("col", "depth"))),
        check_vma=False,
    )
```

```python
import jax
import jax.numpy as jnp
from jax import lax
from jax.experimental import pallas as pl
from jax.experimental.pallas import tpu as pltpu
from jax.sharding import PartitionSpec as P


SN = 256
BLK = 128
NSN = 3
PIV = SN * NSN
ROWS = 16
COLS = 8
CHIPS = 8
XS = 4


def split(a):
    high = a.astype(jnp.bfloat16)
    low = (a - high.astype(jnp.float32)).astype(jnp.bfloat16)
    return high, low


def mul(a, b):
    return jnp.dot(a, b, preferred_element_type=jnp.float32)


def stack(a):
    return jnp.concatenate(split(a), axis=0)


def dot3(a, b):
    rows = a.shape[0] // 2
    both = mul(a, b[0])
    return both[:rows] + (both[rows:] + mul(a[:rows], b[1]))


def inverse(block):
    shape = block.shape
    eye = lax.broadcasted_iota(jnp.int32, shape, 0) == lax.broadcasted_iota(jnp.int32, shape, 1)
    diagonal = jnp.where(eye, block, 0.0)
    by_row = 1.0 / jnp.sum(diagonal, axis=1, keepdims=True)
    by_col = 1.0 / jnp.sum(diagonal, axis=0, keepdims=True)
    power = jnp.where(eye, 0.0, -block * by_row)
    total = jnp.where(eye, 1.0, power)
    for _ in range(5):
        parts = split(power)
        power = dot3(jnp.concatenate(parts, axis=0), parts)
        total = total + dot3(stack(total), split(power))
    return total * by_col


def place_rows(target, own, other, info, columns=slice(None)):
    x, core = info[0], info[1]
    for parts, c in ((own, core), (other, 1 - core)):
        for k in range(XS):
            for e in range(2):
                chip = 2 * lax.rem(x + k, XS) + e
                target[pl.ds(pl.multiple_of(512 * c + 32 * chip, 32), 32), :] = parts[k][48 * e:48 * e + 32, columns]
                target[pl.ds(pl.multiple_of(256 + 128 * c + 16 * chip, 16), 16), :] = parts[k][48 * e + 32:48 * e + 48, columns]


def pieces_kernel(info, front, kept, moved, *out):
    first = info[1] == 0
    for q in range(CHIPS):
        high = front[32 * q:32 * q + 32, :] * kept[q // 4:q // 4 + 1, :]
        mine = front[256 + 16 * q:272 + 16 * q, :] * kept[2:3, :]
        low = jnp.where(first, mine, moved[16 * q:16 * q + 16, :])
        for target in (out[q], out[CHIPS + q]):
            width = target.shape[1]
            target[:32, :] = high[:, :width]
            target[32:, :] = low[:, :width]


def with_ones(info, value, i):
    row_ids = lax.broadcasted_iota(jnp.int32, (SN, SN), 0)
    col_ids = lax.broadcasted_iota(jnp.int32, (SN, SN), 1)
    return jnp.where((row_ids == col_ids) & (row_ids >= info[4 + i]), 1.0, value)


def put_pair(target, pair):
    target[:SN] = pair[0]
    target[SN:] = pair[1]


def factor_first(info, *refs):
    done, rest, matrix = refs[8:]
    place_rows(matrix, refs[:4], refs[4:8], info)
    row_ids = lax.broadcasted_iota(jnp.int32, (SN, SN), 0)
    col_ids = lax.broadcasted_iota(jnp.int32, (SN, SN), 1)

    def block(i, j):
        keep = (row_ids < info[4 + i]) & (col_ids < info[4 + j])
        return jnp.where(keep, matrix[SN * i:SN * i + SN, SN * j:SN * j + SN], 0.0)

    i0 = stack(inverse(with_ones(info, block(0, 0), 0)))
    v01 = split(dot3(i0, split(block(0, 1))))
    v02 = split(dot3(i0, split(block(0, 2))))
    m10 = stack(block(1, 0))
    m20 = stack(block(2, 0))
    done[0] = i0
    done[1] = m10
    done[2] = m20
    put_pair(done.at[3], v01)
    put_pair(done.at[4], v02)
    rest[0] = block(1, 1) - dot3(m10, v01)
    rest[1] = block(1, 2) - dot3(m10, v02)
    rest[2] = block(2, 1) - dot3(m20, v01)
    rest[3] = block(2, 2) - dot3(m20, v02)


def factor_second(info, rest, done, last):
    i1 = stack(inverse(with_ones(info, rest[0], 1)))
    v12 = split(dot3(i1, split(rest[1])))
    m21 = stack(rest[2])
    done[0] = i1
    done[1] = m21
    put_pair(done.at[2], v12)
    last[...] = rest[3] - dot3(m21, v12)


def factor_third(info, last, done):
    done[...] = stack(inverse(with_ones(info, last[...], 2)))


def order_of(info, offset, axis, shape):
    ids = offset + lax.broadcasted_iota(jnp.int32, shape, axis)
    order = jnp.full(shape, NSN, jnp.int32)
    for s in range(NSN):
        order = jnp.where((ids >= SN * s) & (ids < SN * s + info[4 + s]), s, order)
    return order


def left_of(info, strips, first, second, left, panel):
    def pair(block):
        return block[:SN], block[SN:]

    z = info[2]
    for k in range(COLS):
        place = lax.rem(z + k, COLS) * 64
        if k == 4:
            panel[pl.ds(pl.multiple_of(place, 64), 32), :] = strips[4][...]
            panel[pl.ds(pl.multiple_of(place + 32, 32), 32), :] = strips[5][...]
        else:
            panel[pl.ds(pl.multiple_of(place, 64), 64), :] = strips[k if k < 4 else k + 1][...]
    keep = lax.broadcasted_iota(jnp.int32, (512, SN), 1)
    order = order_of(info, info[3] * 512, 0, (512, 1))
    c = [jnp.where(keep < info[4 + s], panel[:, SN * s:SN * s + SN], 0.0) for s in range(NSN)]
    l0 = stack(c[0])
    l1 = stack(c[1] - dot3(l0, pair(first[3])))
    l2 = stack(c[2] - dot3(l0, pair(first[4])) - dot3(l1, pair(second[2])))
    live = jnp.concatenate([order, order], axis=0)
    for s, value in enumerate((l0, l1, l2)):
        left[:, SN * s:SN * s + SN] = jnp.where(live > s, value, jnp.zeros_like(value))


def update_kernel(info, front, kept, *refs, again):
    own, other, (first, second, third) = refs[:4], refs[4:8], refs[8:11]
    step = pl.program_id(0)
    if again:
        left, _, out, quarter, band = refs[11:]
    else:
        strips, (out, quarter, left, band, panel) = refs[11:20], refs[20:]

        @pl.when(step == 0)
        def _():
            left_of(info, strips, first, second, left, panel)

    half = info[8] if again else info[7]
    width = band.shape[1]
    columns = pl.ds(pl.multiple_of(half * 512 + step * width, width), width)
    place_rows(band, own, other, info, columns)
    keep = lax.broadcasted_iota(jnp.int32, (SN, width), 0)
    r = [jnp.where(keep < info[4 + s], band[SN * s:SN * s + SN, :], 0.0) for s in range(NSN)]
    s0 = split(dot3(first[0], split(r[0])))
    s1 = split(dot3(second[0], split(r[1] - dot3(first[1], s0))))
    s2 = split(dot3(third[...], split(r[2] - dot3(first[2], s0) - dot3(second[1], s1))))
    order = order_of(info, info[2] * 1024 + half * 512 + step * width, 1, (1, width))
    total = None
    for s, value in enumerate((s0, s1, s2)):
        live = order > s
        masked = tuple(jnp.where(live, part, jnp.zeros_like(part)) for part in value)
        term = dot3(left[:, SN * s:SN * s + SN], masked)
        total = term if total is None else total + term
    for i in range(4):
        rows = slice(128 * i, 128 * i + 128)
        result = front[rows, :] * kept[i:i + 1, columns] - total[rows]
        out[rows, :] = result
        if i % 2:
            quarter[64 * (i - 1):64 * (i + 1), :] = result[:, 128:]


VMEM_WHOLE = pl.BlockSpec(memory_space=pltpu.VMEM)


def each(axis_size, target):
    return [(i, target(i)) for i in range(axis_size)]


X_UP = each(ROWS, lambda i: (i + 4) % ROWS)
X_DOWN = each(ROWS, lambda i: (i - 4) % ROWS)
MATE = each(ROWS, lambda i: i ^ 2)
CORE = each(ROWS, lambda i: i ^ 1)
Z_UP = each(COLS, lambda i: (i + 1) % COLS)
Z_DOWN = each(COLS, lambda i: (i - 1) % COLS)
Z_ODD = [(z, z + 1) for z in range(0, COLS, 2)]


def gather_plane(piece, odd):
    height = piece.shape[0]
    mate = lax.ppermute(piece, "row", MATE)
    pair = jnp.concatenate([jnp.where(odd, mate, piece), jnp.where(odd, piece, mate)])
    before = lax.ppermute(pair, "row", X_UP)
    after = lax.ppermute(pair, "row", X_DOWN)
    far_even = lax.ppermute(before[:height], "row", X_UP)
    far_odd = lax.ppermute(after[height:], "row", X_DOWN)
    own = [pair, after, jnp.concatenate([far_even, far_odd]), before]
    return own, [lax.ppermute(part, "row", CORE) for part in own]


def gather_line(piece):
    half = piece.shape[0] // 2
    before, after = [piece], [piece]
    for _ in range(1, 4):
        before.append(lax.ppermute(before[-1], "col", Z_UP))
        after.append(lax.ppermute(after[-1], "col", Z_DOWN))
    far_high = lax.ppermute(before[3][:half], "col", Z_UP)
    far_low = lax.ppermute(after[3][half:], "col", Z_DOWN)
    return after[:4] + [far_high, far_low] + before[3:0:-1]


def exchange(front, kept, info, row_index, col_index):
    odd = (row_index // 2) % 2 == 1
    odd_col = col_index % 2 == 1
    moved = lax.ppermute(front[384:512] * kept[3:4], "row", [(0, 1)])
    pieces = pl.pallas_call(
        pieces_kernel,
        grid_spec=pltpu.PrefetchScalarGridSpec(
            num_scalar_prefetch=1,
            grid=(),
            in_specs=[VMEM_WHOLE] * 3,
            out_specs=[VMEM_WHOLE] * (2 * CHIPS),
        ),
        out_shape=[jax.ShapeDtypeStruct((48, width), jnp.float32) for width in [1024] * CHIPS + [PIV] * CHIPS],
        name="pieces",
    )(info, front, kept, moved)

    def from_first(parts):
        return jnp.where(row_index < 2, parts[0], sum(parts[2:], parts[1]))

    pairs = lambda q: [(0, 2 * q * COLS), (COLS, (2 * q + 1) * COLS)]
    parts = [lax.ppermute(pieces[CHIPS + q], ("row", "col"), pairs(q)) for q in range(1, CHIPS)]
    core_piece = from_first([pieces[CHIPS]] + parts)
    parts = [lax.ppermute(core_piece, "col", [(0, z)]) for z in (2, 4, 6)]
    pivot_piece = jnp.where(col_index == 0, core_piece, parts[0] + parts[1] + parts[2])
    pivot_piece = jnp.where(odd_col, lax.ppermute(pivot_piece, "col", Z_ODD), pivot_piece)

    strips = [front[128 * n:128 * n + 128, :PIV] * kept[n:n + 1, :PIV] for n in range(4)]
    parts = [lax.ppermute(strips[n], "col", [(0, 2 * n)]) for n in range(1, 4)]
    strip = jnp.where(col_index == 0, strips[0], parts[0] + parts[1] + parts[2])
    strip = jnp.where(odd_col, lax.ppermute(strip[64:], "col", Z_ODD), strip[:64])

    parts = [lax.ppermute(pieces[q], "row", [(0, 2 * q), (1, 2 * q + 1)]) for q in range(1, CHIPS)]
    piece = from_first([pieces[0]] + parts)

    return gather_plane(piece, odd), gather_plane(pivot_piece, odd), gather_line(strip)


def factor(kernel, inputs, outputs, scratch=()):
    return pl.pallas_call(
        kernel,
        grid_spec=pltpu.PrefetchScalarGridSpec(
            num_scalar_prefetch=1,
            grid=(),
            in_specs=[VMEM_WHOLE] * (len(inputs) - 1),
            out_specs=[VMEM_WHOLE] * len(outputs),
            scratch_shapes=scratch,
        ),
        out_shape=outputs,
        name="factor",
    )(*inputs)


def compute(info, front, kept, band, pivot, strips):
    stacked = lambda *n: jax.ShapeDtypeStruct((*n, 2 * SN, SN), jnp.bfloat16)
    square = lambda *n: jax.ShapeDtypeStruct((*n, SN, SN), jnp.float32)
    first, rest = factor(
        factor_first, (info, *pivot[0], *pivot[1]), [stacked(5), square(4)], [pltpu.VMEM((PIV, PIV), jnp.float32)]
    )
    second, last = factor(factor_second, (info, rest), [stacked(3), square()])
    (third,) = factor(factor_third, (info, last), [stacked()])
    width = 256

    def update(which, *inputs):
        def at(j, info):
            return (0, info[7 + which] * 2 + j)

        left_shape = (1024, PIV)
        specs = [VMEM_WHOLE, pl.BlockSpec(memory_space=pl.ANY)] if which else [VMEM_WHOLE] * len(inputs)
        return pl.pallas_call(
            lambda *refs: update_kernel(*refs, again=which == 1),
            grid_spec=pltpu.PrefetchScalarGridSpec(
                num_scalar_prefetch=1,
                grid=(2,),
                in_specs=[pl.BlockSpec((512, width), at)] + [VMEM_WHOLE] * 12 + specs,
                out_specs=[
                    pl.BlockSpec((512, width), at),
                    pl.BlockSpec((256, width // 2), lambda j, info: (0, j)),
                ] + [VMEM_WHOLE] * (1 - which),
                scratch_shapes=[pltpu.VMEM((PIV, width), jnp.float32)] + [pltpu.VMEM((512, PIV), jnp.float32)] * (1 - which),
            ),
            out_shape=[
                jax.ShapeDtypeStruct((512, 1024), jnp.float32),
                jax.ShapeDtypeStruct((256, 256), jnp.float32),
            ] + [jax.ShapeDtypeStruct(left_shape, jnp.bfloat16)] * (1 - which),
            input_output_aliases={15: 0} if which else {},
            name="update",
        )(info, front, kept, *band[0], *band[1], first, second, third, *inputs)

    partial, leaving, left = update(0, *strips)
    arriving = lax.ppermute(leaving, "depth", [(0, 1), (1, 0)])
    result, staying = update(1, left, partial)
    return result[None], staying + arriving


def local(front_matrix, block_mask, supernode_width):
    row_index = lax.axis_index("row")
    col_index = lax.axis_index("col")
    depth_index = lax.axis_index("depth")
    block_rows = row_index * 4 + jnp.arange(4)
    block_cols = col_index * 8 + jnp.arange(8)
    kept = ((block_mask[0] != 0) | (block_rows[:, None] == block_cols[None, :])).astype(jnp.float32)
    kept = jnp.broadcast_to(kept[:, :, None], (4, 8, BLK)).reshape(4, 1024)
    front = front_matrix[0]
    info = jnp.concatenate([
        jnp.stack([row_index // 4, row_index % 2, col_index, row_index]).astype(jnp.int32),
        supernode_width[0],
        jnp.stack([1 - depth_index, depth_index]).astype(jnp.int32),
    ])
    panels = exchange(front, kept, info, row_index, col_index)
    return compute(info, front, kept, *panels)


def solution(mesh):
    placed = (P("depth", "row", "col"), P("depth", "row", "col"), P("depth", None))
    return jax.shard_map(
        local,
        mesh=mesh,
        in_specs=placed,
        out_specs=(P("depth", "row", "col"), P("row", ("col", "depth"))),
        check_vma=False,
    )
```

```python
import jax
import jax.numpy as jnp
from jax import lax
from jax.experimental import pallas as pl
from jax.experimental.pallas import tpu as pltpu
from jax.sharding import PartitionSpec as P


SN = 256
BLK = 128
NSN = 3
PIV = SN * NSN
ROWS = 16
COLS = 8
CHIPS = 8
XS = 4


def split(a):
    high = a.astype(jnp.bfloat16)
    low = (a - high.astype(jnp.float32)).astype(jnp.bfloat16)
    return high, low


def mul(a, b):
    return jnp.dot(a, b, preferred_element_type=jnp.float32)


def stack(a):
    return jnp.concatenate(split(a), axis=0)


def dot3(a, b):
    rows = a.shape[0] // 2
    both = mul(a, b[0])
    return both[:rows] + (both[rows:] + mul(a[:rows], b[1]))


def inverse(block):
    shape = block.shape
    eye = lax.broadcasted_iota(jnp.int32, shape, 0) == lax.broadcasted_iota(jnp.int32, shape, 1)
    diagonal = jnp.where(eye, block, 0.0)
    by_row = 1.0 / jnp.sum(diagonal, axis=1, keepdims=True)
    by_col = 1.0 / jnp.sum(diagonal, axis=0, keepdims=True)
    power = jnp.where(eye, 0.0, -block * by_row)
    total = jnp.where(eye, 1.0, power)
    for _ in range(5):
        parts = split(power)
        power = dot3(jnp.concatenate(parts, axis=0), parts)
        total = total + dot3(stack(total), split(power))
    return total * by_col


def place_rows(target, own, other, info, columns=slice(None)):
    x, core = info[0], info[1]
    for parts, c in ((own, core), (other, 1 - core)):
        for k in range(XS):
            for e in range(2):
                chip = 2 * lax.rem(x + k, XS) + e
                target[pl.ds(pl.multiple_of(512 * c + 32 * chip, 32), 32), :] = parts[k][48 * e:48 * e + 32, columns]
                target[pl.ds(pl.multiple_of(256 + 128 * c + 16 * chip, 16), 16), :] = parts[k][48 * e + 32:48 * e + 48, columns]


def pieces_kernel(info, front, kept, moved, *out):
    first = info[1] == 0
    for q in range(CHIPS):
        out[q][:32, :] = front[32 * q:32 * q + 32, :] * kept[q // 4:q // 4 + 1, :]
        mine = front[256 + 16 * q:272 + 16 * q, :] * kept[2:3, :]
        out[q][32:, :] = jnp.where(first, mine, moved[16 * q:16 * q + 16, :])


def with_ones(info, value, i):
    row_ids = lax.broadcasted_iota(jnp.int32, (SN, SN), 0)
    col_ids = lax.broadcasted_iota(jnp.int32, (SN, SN), 1)
    return jnp.where((row_ids == col_ids) & (row_ids >= info[4 + i]), 1.0, value)


def put_pair(target, pair):
    target[:SN] = pair[0]
    target[SN:] = pair[1]


def factor_first(info, *refs):
    done, rest, matrix = refs[8:]
    place_rows(matrix, refs[:4], refs[4:8], info)
    row_ids = lax.broadcasted_iota(jnp.int32, (SN, SN), 0)
    col_ids = lax.broadcasted_iota(jnp.int32, (SN, SN), 1)

    def block(i, j):
        keep = (row_ids < info[4 + i]) & (col_ids < info[4 + j])
        return jnp.where(keep, matrix[SN * i:SN * i + SN, SN * j:SN * j + SN], 0.0)

    i0 = stack(inverse(with_ones(info, block(0, 0), 0)))
    v01 = split(dot3(i0, split(block(0, 1))))
    v02 = split(dot3(i0, split(block(0, 2))))
    m10 = stack(block(1, 0))
    m20 = stack(block(2, 0))
    done[0] = i0
    done[1] = m10
    done[2] = m20
    put_pair(done.at[3], v01)
    put_pair(done.at[4], v02)
    rest[0] = block(1, 1) - dot3(m10, v01)
    rest[1] = block(1, 2) - dot3(m10, v02)
    rest[2] = block(2, 1) - dot3(m20, v01)
    rest[3] = block(2, 2) - dot3(m20, v02)


def factor_second(info, rest, done, last):
    i1 = stack(inverse(with_ones(info, rest[0], 1)))
    v12 = split(dot3(i1, split(rest[1])))
    m21 = stack(rest[2])
    done[0] = i1
    done[1] = m21
    put_pair(done.at[2], v12)
    last[...] = rest[3] - dot3(m21, v12)


def factor_third(info, last, done):
    done[...] = stack(inverse(with_ones(info, last[...], 2)))


def factor_kernel(info, *refs):
    first, second, third, rest, last, matrix = refs[8:]
    factor_first(info, *refs[:8], first, rest, matrix)
    factor_second(info, rest, second, last)
    factor_third(info, last, third)


def order_of(info, offset, axis, shape):
    ids = offset + lax.broadcasted_iota(jnp.int32, shape, axis)
    order = jnp.full(shape, NSN, jnp.int32)
    for s in range(NSN):
        order = jnp.where((ids >= SN * s) & (ids < SN * s + info[4 + s]), s, order)
    return order


def left_of(info, panel, first, second, left):
    def pair(block):
        return block[:SN], block[SN:]

    keep = lax.broadcasted_iota(jnp.int32, (512, SN), 1)
    order = order_of(info, info[3] * 512, 0, (512, 1))
    c = [jnp.where(keep < info[4 + s], panel[:, SN * s:SN * s + SN], 0.0) for s in range(NSN)]
    l0 = stack(c[0])
    l1 = stack(c[1] - dot3(l0, pair(first[3])))
    l2 = stack(c[2] - dot3(l0, pair(first[4])) - dot3(l1, pair(second[2])))
    live = jnp.concatenate([order, order], axis=0)
    for s, value in enumerate((l0, l1, l2)):
        left[:, SN * s:SN * s + SN] = jnp.where(live > s, value, jnp.zeros_like(value))


def update_kernel(info, front, kept, *refs, again):
    own, other, (first, second, third) = refs[:4], refs[4:8], refs[8:11]
    step = pl.program_id(0)
    if again:
        left, _, out, quarter, band = refs[11:]
    else:
        panel, out, quarter, left, band = refs[11:]

        @pl.when(step == 0)
        def _():
            left_of(info, panel, first, second, left)

    half = info[8] if again else info[7]
    width = band.shape[1]
    columns = pl.ds(pl.multiple_of(half * 512 + step * width, width), width)
    place_rows(band, own, other, info, columns)
    keep = lax.broadcasted_iota(jnp.int32, (SN, width), 0)
    r = [jnp.where(keep < info[4 + s], band[SN * s:SN * s + SN, :], 0.0) for s in range(NSN)]
    s0 = split(dot3(first[0], split(r[0])))
    s1 = split(dot3(second[0], split(r[1] - dot3(first[1], s0))))
    s2 = split(dot3(third[...], split(r[2] - dot3(first[2], s0) - dot3(second[1], s1))))
    order = order_of(info, info[2] * 1024 + half * 512 + step * width, 1, (1, width))
    total = None
    for s, value in enumerate((s0, s1, s2)):
        live = order > s
        masked = tuple(jnp.where(live, part, jnp.zeros_like(part)) for part in value)
        term = dot3(left[:, SN * s:SN * s + SN], masked)
        total = term if total is None else total + term
    for i in range(4):
        rows = slice(128 * i, 128 * i + 128)
        result = front[rows, :] * kept[i:i + 1, columns] - total[rows]
        out[rows, :] = result
        if i % 2:
            quarter[64 * (i - 1):64 * (i + 1), :] = result[:, 128:]


VMEM_WHOLE = pl.BlockSpec(memory_space=pltpu.VMEM)


def each(axis_size, target):
    return [(i, target(i)) for i in range(axis_size)]


X_UP = each(ROWS, lambda i: (i + 4) % ROWS)
X_DOWN = each(ROWS, lambda i: (i - 4) % ROWS)
MATE = each(ROWS, lambda i: i ^ 2)
CORE = each(ROWS, lambda i: i ^ 1)
Z_ODD = [(z, z + 1) for z in range(0, COLS, 2)]


def gather_plane(piece, odd):
    height = piece.shape[0]
    mate = lax.ppermute(piece, "row", MATE)
    pair = jnp.concatenate([jnp.where(odd, mate, piece), jnp.where(odd, piece, mate)])
    before = lax.ppermute(pair, "row", X_UP)
    after = lax.ppermute(pair, "row", X_DOWN)
    far_even = lax.ppermute(before[:height], "row", X_UP)
    far_odd = lax.ppermute(after[height:], "row", X_DOWN)
    own = [pair, after, jnp.concatenate([far_even, far_odd]), before]
    return own, [lax.ppermute(part, "row", CORE) for part in own]


def exchange(front, kept, info, row_index, col_index):
    odd = (row_index // 2) % 2 == 1
    odd_col = col_index % 2 == 1
    moved = lax.ppermute(front[384:512] * kept[3:4], "row", [(0, 1)])
    pieces = pl.pallas_call(
        pieces_kernel,
        grid_spec=pltpu.PrefetchScalarGridSpec(
            num_scalar_prefetch=1,
            grid=(),
            in_specs=[VMEM_WHOLE] * 3,
            out_specs=[VMEM_WHOLE] * CHIPS,
        ),
        out_shape=[jax.ShapeDtypeStruct((48, 1024), jnp.float32)] * CHIPS,
        name="pieces",
    )(info, front, kept, moved)
    parts = [lax.ppermute(pieces[q], "row", [(0, 2 * q), (1, 2 * q + 1)]) for q in range(1, CHIPS)]
    piece = jnp.where(row_index < 2, pieces[0], sum(parts[1:], parts[0]))

    core_piece = piece[:, :PIV]
    parts = [lax.ppermute(core_piece, "col", [(0, z)]) for z in (2, 4, 6)]
    pivot_piece = jnp.where(col_index == 0, core_piece, parts[0] + parts[1] + parts[2])
    pivot_piece = jnp.where(odd_col, lax.ppermute(pivot_piece, "col", Z_ODD), pivot_piece)

    strips = [front[64 * z:64 * z + 64, :PIV] * kept[z // 2:z // 2 + 1, :PIV] for z in range(COLS)]
    parts = [lax.ppermute(strips[z], "col", [(0, z)]) for z in range(1, COLS)]
    strip = jnp.where(col_index == 0, strips[0], sum(parts[1:], parts[0]))
    panel = lax.all_to_all(jnp.broadcast_to(strip[None], (COLS, 64, PIV)), "col", 0, 0).reshape(512, PIV)

    return gather_plane(piece, odd), gather_plane(pivot_piece, odd), panel


def compute(info, front, kept, band, pivot, panel):
    stacked = lambda *n: jax.ShapeDtypeStruct((*n, 2 * SN, SN), jnp.bfloat16)
    first, second, third = pl.pallas_call(
        factor_kernel,
        grid_spec=pltpu.PrefetchScalarGridSpec(
            num_scalar_prefetch=1,
            grid=(),
            in_specs=[VMEM_WHOLE] * 8,
            out_specs=[VMEM_WHOLE] * 3,
            scratch_shapes=[
                pltpu.VMEM((4, SN, SN), jnp.float32),
                pltpu.VMEM((SN, SN), jnp.float32),
                pltpu.VMEM((PIV, PIV), jnp.float32),
            ],
        ),
        out_shape=[stacked(5), stacked(3), stacked()],
        name="factor",
    )(info, *pivot[0], *pivot[1])
    width = 256

    def update(which, *inputs):
        def at(j, info):
            return (0, info[7 + which] * 2 + j)

        left_shape = (1024, PIV)
        specs = [VMEM_WHOLE, pl.BlockSpec(memory_space=pl.ANY)] if which else [VMEM_WHOLE] * len(inputs)
        return pl.pallas_call(
            lambda *refs: update_kernel(*refs, again=which == 1),
            grid_spec=pltpu.PrefetchScalarGridSpec(
                num_scalar_prefetch=1,
                grid=(2,),
                in_specs=[pl.BlockSpec((512, width), at)] + [VMEM_WHOLE] * 12 + specs,
                out_specs=[
                    pl.BlockSpec((512, width), at),
                    pl.BlockSpec((256, width // 2), lambda j, info: (0, j)),
                ] + [VMEM_WHOLE] * (1 - which),
                scratch_shapes=[pltpu.VMEM((PIV, width), jnp.float32)],
            ),
            out_shape=[
                jax.ShapeDtypeStruct((512, 1024), jnp.float32),
                jax.ShapeDtypeStruct((256, 256), jnp.float32),
            ] + [jax.ShapeDtypeStruct(left_shape, jnp.bfloat16)] * (1 - which),
            input_output_aliases={15: 0} if which else {},
            name="update",
        )(info, front, kept, *band[0], *band[1], first, second, third, *inputs)

    partial, leaving, left = update(0, panel)
    arriving = lax.ppermute(leaving, "depth", [(0, 1), (1, 0)])
    result, staying = update(1, left, partial)
    return result[None], staying + arriving


def local(front_matrix, block_mask, supernode_width):
    row_index = lax.axis_index("row")
    col_index = lax.axis_index("col")
    depth_index = lax.axis_index("depth")
    block_rows = row_index * 4 + jnp.arange(4)
    block_cols = col_index * 8 + jnp.arange(8)
    kept = ((block_mask[0] != 0) | (block_rows[:, None] == block_cols[None, :])).astype(jnp.float32)
    kept = jnp.broadcast_to(kept[:, :, None], (4, 8, BLK)).reshape(4, 1024)
    front = front_matrix[0]
    info = jnp.concatenate([
        jnp.stack([row_index // 4, row_index % 2, col_index, row_index]).astype(jnp.int32),
        supernode_width[0],
        jnp.stack([1 - depth_index, depth_index]).astype(jnp.int32),
    ])
    panels = exchange(front, kept, info, row_index, col_index)
    return compute(info, front, kept, *panels)


def solution(mesh):
    placed = (P("depth", "row", "col"), P("depth", "row", "col"), P("depth", None))
    return jax.shard_map(
        local,
        mesh=mesh,
        in_specs=placed,
        out_specs=(P("depth", "row", "col"), P("row", ("col", "depth"))),
        check_vma=False,
    )
```

```python
import jax
import jax.numpy as jnp
from jax import lax
from jax.experimental import pallas as pl
from jax.experimental.pallas import tpu as pltpu
from jax.sharding import PartitionSpec as P


SN = 256
BLK = 128
NSN = 3
PIV = SN * NSN
ROWS = 16
COLS = 8
CHIPS = 8
XS = 4


def split(a):
    high = a.astype(jnp.bfloat16)
    low = (a - high.astype(jnp.float32)).astype(jnp.bfloat16)
    return high, low


def mul(a, b):
    return jnp.dot(a, b, preferred_element_type=jnp.float32)


def stack(a):
    return jnp.concatenate(split(a), axis=0)


def dot3(a, b):
    rows = a.shape[0] // 2
    both = mul(a, b[0])
    return both[:rows] + (both[rows:] + mul(a[:rows], b[1]))


def inverse(block):
    shape = block.shape
    eye = lax.broadcasted_iota(jnp.int32, shape, 0) == lax.broadcasted_iota(jnp.int32, shape, 1)
    diagonal = jnp.where(eye, block, 0.0)
    by_row = 1.0 / jnp.sum(diagonal, axis=1, keepdims=True)
    by_col = 1.0 / jnp.sum(diagonal, axis=0, keepdims=True)
    power = jnp.where(eye, 0.0, -block * by_row)
    total = jnp.where(eye, 1.0, power)
    for _ in range(5):
        parts = split(power)
        power = dot3(jnp.concatenate(parts, axis=0), parts)
        total = total + dot3(stack(total), split(power))
    return total * by_col


def place_rows(target, own, other, info, columns=slice(None)):
    x, core = info[0], info[1]
    for parts, c in ((own, core), (other, 1 - core)):
        for k in range(XS):
            for e in range(2):
                chip = 2 * lax.rem(x + k, XS) + e
                target[pl.ds(pl.multiple_of(512 * c + 32 * chip, 32), 32), :] = parts[k][48 * e:48 * e + 32, columns]
                target[pl.ds(pl.multiple_of(256 + 128 * c + 16 * chip, 16), 16), :] = parts[k][48 * e + 32:48 * e + 48, columns]


def pieces_kernel(info, front, kept, moved, *out):
    first = info[1] == 0
    for q in range(CHIPS):
        out[q][:32, :] = front[32 * q:32 * q + 32, :] * kept[q // 4:q // 4 + 1, :]
        mine = front[256 + 16 * q:272 + 16 * q, :] * kept[2:3, :]
        out[q][32:, :] = jnp.where(first, mine, moved[16 * q:16 * q + 16, :])


def with_ones(info, value, i):
    row_ids = lax.broadcasted_iota(jnp.int32, (SN, SN), 0)
    col_ids = lax.broadcasted_iota(jnp.int32, (SN, SN), 1)
    return jnp.where((row_ids == col_ids) & (row_ids >= info[4 + i]), 1.0, value)


def put_pair(target, pair):
    target[:SN] = pair[0]
    target[SN:] = pair[1]


def factor_kernel(info, *refs):
    lower, upper, matrix = refs[8:]
    place_rows(matrix, refs[:4], refs[4:8], info)
    row_ids = lax.broadcasted_iota(jnp.int32, (SN, SN), 0)
    col_ids = lax.broadcasted_iota(jnp.int32, (SN, SN), 1)

    def block(i, j):
        keep = (row_ids < info[4 + i]) & (col_ids < info[4 + j])
        return jnp.where(keep, matrix[SN * i:SN * i + SN, SN * j:SN * j + SN], 0.0)

    i0 = inverse(with_ones(info, block(0, 0), 0))
    i0_parts, i0 = split(i0), stack(i0)
    v01 = dot3(i0, split(block(0, 1)))
    v02 = dot3(i0, split(block(0, 2)))
    v01_parts, v02_parts = split(v01), split(v02)
    m10 = stack(block(1, 0))
    m20 = stack(block(2, 0))
    i1 = inverse(with_ones(info, block(1, 1) - dot3(m10, v01_parts), 1))
    i1_parts, i1 = split(i1), stack(i1)
    m21 = stack(block(2, 1) - dot3(m20, v01_parts))
    v12 = split(dot3(i1, split(block(1, 2) - dot3(m10, v02_parts))))
    i2 = stack(inverse(with_ones(info, block(2, 2) - dot3(m20, v02_parts) - dot3(m21, v12), 2)))
    g10 = -dot3(i1, split(dot3(m10, i0_parts)))
    h20 = split(dot3(m20, i0_parts) + dot3(m21, split(g10)))
    h21 = split(dot3(m21, i1_parts))
    lower[0] = i0
    lower[1] = stack(g10)
    lower[2] = i1
    lower[3] = stack(-dot3(i2, h20))
    lower[4] = stack(-dot3(i2, h21))
    lower[5] = i2
    put_pair(upper.at[0], v01_parts)
    put_pair(upper.at[1], v12)
    put_pair(upper.at[2], split(v02 - dot3(stack(v01), v12)))


def order_of(info, offset, axis, shape):
    ids = offset + lax.broadcasted_iota(jnp.int32, shape, axis)
    order = jnp.full(shape, NSN, jnp.int32)
    for s in range(NSN):
        order = jnp.where((ids >= SN * s) & (ids < SN * s + info[4 + s]), s, order)
    return order


def left_of(info, panel, upper, left):
    def pair(n):
        return upper[n, :SN], upper[n, SN:]

    keep = lax.broadcasted_iota(jnp.int32, (512, SN), 1)
    order = order_of(info, info[3] * 512, 0, (512, 1))
    c = [jnp.where(keep < info[4 + s], panel[:, SN * s:SN * s + SN], 0.0) for s in range(NSN)]
    c0, c1 = stack(c[0]), stack(c[1])
    l1 = stack(c[1] - dot3(c0, pair(0)))
    l2 = stack(c[2] - dot3(c0, pair(2)) - dot3(c1, pair(1)))
    live = jnp.concatenate([order, order], axis=0)
    for s, value in enumerate((c0, l1, l2)):
        left[:, SN * s:SN * s + SN] = jnp.where(live > s, value, jnp.zeros_like(value))


def update_kernel(info, front, kept, *refs, again):
    own, other, lower = refs[:4], refs[4:8], refs[8]
    if again:
        left, _, out, quarter, band, block, sems = refs[9:]
    else:
        upper, panel, out, quarter, left, band, block, sems = refs[9:]
        left_of(info, panel, upper, left)
    half = info[8] if again else info[7]
    width = band.shape[1]
    columns = pl.ds(pl.multiple_of(half * 512, 512), 512)
    place_rows(band, own, other, info, columns)
    keep = lax.broadcasted_iota(jnp.int32, (SN, width), 0)
    r = [split(jnp.where(keep < info[4 + s], band[SN * s:SN * s + SN, :], 0.0)) for s in range(NSN)]
    s0 = split(dot3(lower[0], r[0]))
    s1 = split(dot3(lower[1], r[0]) + dot3(lower[2], r[1]))
    s2 = split(dot3(lower[3], r[0]) + dot3(lower[4], r[1]) + dot3(lower[5], r[2]))
    order = order_of(info, info[2] * 1024 + half * 512, 1, (1, width))
    total = None
    for s, value in enumerate((s0, s1, s2)):
        live = order > s
        masked = tuple(jnp.where(live, part, jnp.zeros_like(part)) for part in value)
        term = dot3(left[:, SN * s:SN * s + SN], masked)
        total = term if total is None else total + term
    copies = []
    for i in range(4):
        rows = slice(128 * i, 128 * i + 128)
        result = front[rows, columns] * kept[i:i + 1, columns] - total[rows]
        block[rows, :] = result
        copies.append(pltpu.make_async_copy(block.at[rows, :], out.at[rows, columns], sems.at[i]))
        copies[i].start()
        if i % 2:
            for j in range(2):
                quarter[64 * (i - 1):64 * (i + 1), 128 * j:128 * j + 128] = result[:, 256 * j + 128:256 * j + 256]
    for copy in copies:
        copy.wait()


VMEM_WHOLE = pl.BlockSpec(memory_space=pltpu.VMEM)


def each(axis_size, target):
    return [(i, target(i)) for i in range(axis_size)]


X_UP = each(ROWS, lambda i: (i + 4) % ROWS)
X_DOWN = each(ROWS, lambda i: (i - 4) % ROWS)
MATE = each(ROWS, lambda i: i ^ 2)
CORE = each(ROWS, lambda i: i ^ 1)
Z_ODD = [(z, z + 1) for z in range(0, COLS, 2)]


def gather_plane(piece, odd):
    height = piece.shape[0]
    mate = lax.ppermute(piece, "row", MATE)
    pair = jnp.concatenate([jnp.where(odd, mate, piece), jnp.where(odd, piece, mate)])
    before = lax.ppermute(pair, "row", X_UP)
    after = lax.ppermute(pair, "row", X_DOWN)
    far_even = lax.ppermute(before[:height], "row", X_UP)
    far_odd = lax.ppermute(after[height:], "row", X_DOWN)
    own = [pair, after, jnp.concatenate([far_even, far_odd]), before]
    return own, [lax.ppermute(part, "row", CORE) for part in own]


def exchange(front, kept, info, row_index, col_index):
    odd = (row_index // 2) % 2 == 1
    odd_col = col_index % 2 == 1
    moved = lax.ppermute(front[384:512] * kept[3:4], "row", [(0, 1)])
    pieces = pl.pallas_call(
        pieces_kernel,
        grid_spec=pltpu.PrefetchScalarGridSpec(
            num_scalar_prefetch=1,
            grid=(),
            in_specs=[VMEM_WHOLE] * 3,
            out_specs=[VMEM_WHOLE] * CHIPS,
        ),
        out_shape=[jax.ShapeDtypeStruct((48, 1024), jnp.float32)] * CHIPS,
        name="pieces",
    )(info, front, kept, moved)
    parts = [lax.ppermute(pieces[q], "row", [(0, 2 * q), (1, 2 * q + 1)]) for q in range(1, CHIPS)]
    piece = jnp.where(row_index < 2, pieces[0], sum(parts[1:], parts[0]))

    core_piece = piece[:, :PIV]
    parts = [lax.ppermute(core_piece, "col", [(0, z)]) for z in (2, 4, 6)]
    pivot_piece = jnp.where(col_index == 0, core_piece, parts[0] + parts[1] + parts[2])
    pivot_piece = jnp.where(odd_col, lax.ppermute(pivot_piece, "col", Z_ODD), pivot_piece)

    strips = [front[64 * z:64 * z + 64, :PIV] * kept[z // 2:z // 2 + 1, :PIV] for z in range(COLS)]
    parts = [lax.ppermute(strips[z], "col", [(0, z)]) for z in range(1, COLS)]
    strip = jnp.where(col_index == 0, strips[0], sum(parts[1:], parts[0]))
    panel = lax.all_to_all(jnp.broadcast_to(strip[None], (COLS, 64, PIV)), "col", 0, 0).reshape(512, PIV)

    return gather_plane(piece, odd), gather_plane(pivot_piece, odd), panel


def compute(info, front, kept, band, pivot, panel):
    stacked = lambda *n: jax.ShapeDtypeStruct((*n, 2 * SN, SN), jnp.bfloat16)
    lower, upper = pl.pallas_call(
        factor_kernel,
        grid_spec=pltpu.PrefetchScalarGridSpec(
            num_scalar_prefetch=1,
            grid=(),
            in_specs=[VMEM_WHOLE] * 8,
            out_specs=[VMEM_WHOLE] * 2,
            scratch_shapes=[pltpu.VMEM((PIV, PIV), jnp.float32)],
        ),
        out_shape=[stacked(6), stacked(3)],
        name="factor",
    )(info, *pivot[0], *pivot[1])

    def update(which, *inputs):
        left_shape = (1024, PIV)
        anywhere = pl.BlockSpec(memory_space=pl.ANY)
        specs = [VMEM_WHOLE, anywhere] if which else [VMEM_WHOLE] * len(inputs)
        return pl.pallas_call(
            lambda *refs: update_kernel(*refs, again=which == 1),
            grid_spec=pltpu.PrefetchScalarGridSpec(
                num_scalar_prefetch=1,
                grid=(),
                in_specs=[VMEM_WHOLE] * 11 + specs,
                out_specs=[anywhere, VMEM_WHOLE] + [VMEM_WHOLE] * (1 - which),
                scratch_shapes=[
                    pltpu.VMEM((PIV, 512), jnp.float32),
                    pltpu.VMEM((512, 512), jnp.float32),
                    pltpu.SemaphoreType.DMA((4,)),
                ],
            ),
            out_shape=[
                jax.ShapeDtypeStruct((512, 1024), jnp.float32),
                jax.ShapeDtypeStruct((256, 256), jnp.float32),
            ] + [jax.ShapeDtypeStruct(left_shape, jnp.bfloat16)] * (1 - which),
            input_output_aliases={13: 0} if which else {},
            name="update",
        )(info, front, kept, *band[0], *band[1], lower, *inputs)

    partial, leaving, left = update(0, upper, panel)
    arriving = lax.ppermute(leaving, "depth", [(0, 1), (1, 0)])
    result, staying = update(1, left, partial)
    return result[None], staying + arriving


def local(front_matrix, block_mask, supernode_width):
    row_index = lax.axis_index("row")
    col_index = lax.axis_index("col")
    depth_index = lax.axis_index("depth")
    block_rows = row_index * 4 + jnp.arange(4)
    block_cols = col_index * 8 + jnp.arange(8)
    kept = ((block_mask[0] != 0) | (block_rows[:, None] == block_cols[None, :])).astype(jnp.float32)
    kept = jnp.broadcast_to(kept[:, :, None], (4, 8, BLK)).reshape(4, 1024)
    front = front_matrix[0]
    info = jnp.concatenate([
        jnp.stack([row_index // 4, row_index % 2, col_index, row_index]).astype(jnp.int32),
        supernode_width[0],
        jnp.stack([1 - depth_index, depth_index]).astype(jnp.int32),
    ])
    panels = exchange(front, kept, info, row_index, col_index)
    return compute(info, front, kept, *panels)


def solution(mesh):
    placed = (P("depth", "row", "col"), P("depth", "row", "col"), P("depth", None))
    return jax.shard_map(
        local,
        mesh=mesh,
        in_specs=placed,
        out_specs=(P("depth", "row", "col"), P("row", ("col", "depth"))),
        check_vma=False,
    )
```

```python
import jax
import jax.numpy as jnp
from jax import lax
from jax.experimental import pallas as pl
from jax.experimental.pallas import tpu as pltpu
from jax.sharding import PartitionSpec as P


SN = 256
BLK = 128
NSN = 3
PIV = SN * NSN
ROWS = 16
COLS = 8
CHIPS = 8
XS = 4


def split(a):
    high = a.astype(jnp.bfloat16)
    low = (a - high.astype(jnp.float32)).astype(jnp.bfloat16)
    return high, low


def mul(a, b):
    return jnp.dot(a, b, preferred_element_type=jnp.float32)


def stack(a):
    return jnp.concatenate(split(a), axis=0)


def dot3(a, b):
    rows = a.shape[0] // 2
    both = mul(a, b[0])
    return both[:rows] + (both[rows:] + mul(a[:rows], b[1]))


def inverse(block):
    shape = block.shape
    eye = lax.broadcasted_iota(jnp.int32, shape, 0) == lax.broadcasted_iota(jnp.int32, shape, 1)
    diagonal = jnp.where(eye, block, 0.0)
    by_row = 1.0 / jnp.sum(diagonal, axis=1, keepdims=True)
    by_col = 1.0 / jnp.sum(diagonal, axis=0, keepdims=True)
    power = jnp.where(eye, 0.0, -block * by_row)
    total = jnp.where(eye, 1.0, power)
    for _ in range(5):
        parts = split(power)
        power = dot3(jnp.concatenate(parts, axis=0), parts)
        total = total + dot3(stack(total), split(power))
    return total * by_col


def place_rows(target, own, other, info, columns=slice(None)):
    x, core = info[0], info[1]
    for parts, c in ((own, core), (other, 1 - core)):
        for k in range(XS):
            for e in range(2):
                chip = 2 * lax.rem(x + k, XS) + e
                target[pl.ds(pl.multiple_of(512 * c + 32 * chip, 32), 32), :] = parts[k][48 * e:48 * e + 32, columns]
                target[pl.ds(pl.multiple_of(256 + 128 * c + 16 * chip, 16), 16), :] = parts[k][48 * e + 32:48 * e + 48, columns]


def pieces_kernel(info, front, kept, moved, *out):
    first = info[1] == 0
    for q in range(CHIPS):
        out[q][:32, :] = front[32 * q:32 * q + 32, :] * kept[q // 4:q // 4 + 1, :]
        mine = front[256 + 16 * q:272 + 16 * q, :] * kept[2:3, :]
        out[q][32:, :] = jnp.where(first, mine, moved[16 * q:16 * q + 16, :])


def with_ones(info, value, i):
    row_ids = lax.broadcasted_iota(jnp.int32, (SN, SN), 0)
    col_ids = lax.broadcasted_iota(jnp.int32, (SN, SN), 1)
    return jnp.where((row_ids == col_ids) & (row_ids >= info[4 + i]), 1.0, value)


def put_pair(target, pair):
    target[:SN] = pair[0]
    target[SN:] = pair[1]


def factor_kernel(info, *refs):
    lower, upper, matrix = refs[8:]
    place_rows(matrix, refs[:4], refs[4:8], info)
    row_ids = lax.broadcasted_iota(jnp.int32, (SN, SN), 0)
    col_ids = lax.broadcasted_iota(jnp.int32, (SN, SN), 1)

    def block(i, j):
        keep = (row_ids < info[4 + i]) & (col_ids < info[4 + j])
        return jnp.where(keep, matrix[SN * i:SN * i + SN, SN * j:SN * j + SN], 0.0)

    i0 = inverse(with_ones(info, block(0, 0), 0))
    i0_parts, i0 = split(i0), stack(i0)
    v01 = dot3(i0, split(block(0, 1)))
    v02 = dot3(i0, split(block(0, 2)))
    v01_parts, v02_parts = split(v01), split(v02)
    m10 = stack(block(1, 0))
    m20 = stack(block(2, 0))
    i1 = inverse(with_ones(info, block(1, 1) - dot3(m10, v01_parts), 1))
    i1_parts, i1 = split(i1), stack(i1)
    m21 = stack(block(2, 1) - dot3(m20, v01_parts))
    v12 = split(dot3(i1, split(block(1, 2) - dot3(m10, v02_parts))))
    i2 = stack(inverse(with_ones(info, block(2, 2) - dot3(m20, v02_parts) - dot3(m21, v12), 2)))
    g10 = -dot3(i1, split(dot3(m10, i0_parts)))
    h20 = split(dot3(m20, i0_parts) + dot3(m21, split(g10)))
    h21 = split(dot3(m21, i1_parts))
    lower[0] = i0
    lower[1] = stack(g10)
    lower[2] = i1
    lower[3] = stack(-dot3(i2, h20))
    lower[4] = stack(-dot3(i2, h21))
    lower[5] = i2
    put_pair(upper.at[0], v01_parts)
    put_pair(upper.at[1], v12)
    put_pair(upper.at[2], split(v02 - dot3(stack(v01), v12)))


def order_of(info, offset, axis, shape):
    ids = offset + lax.broadcasted_iota(jnp.int32, shape, axis)
    order = jnp.full(shape, NSN, jnp.int32)
    for s in range(NSN):
        order = jnp.where((ids >= SN * s) & (ids < SN * s + info[4 + s]), s, order)
    return order


def left_of(info, panel, upper, left):
    def pair(n):
        return upper[n, :SN], upper[n, SN:]

    keep = lax.broadcasted_iota(jnp.int32, (512, SN), 1)
    order = order_of(info, info[3] * 512, 0, (512, 1))
    c = [jnp.where(keep < info[4 + s], panel[:, SN * s:SN * s + SN], 0.0) for s in range(NSN)]
    c0, c1 = stack(c[0]), stack(c[1])
    l1 = stack(c[1] - dot3(c0, pair(0)))
    l2 = stack(c[2] - dot3(c0, pair(2)) - dot3(c1, pair(1)))
    live = jnp.concatenate([order, order], axis=0)
    for s, value in enumerate((c0, l1, l2)):
        left[:, SN * s:SN * s + SN] = jnp.where(live > s, value, jnp.zeros_like(value))


def update_kernel(info, front, kept, *refs, again):
    own, other, lower = refs[:4], refs[4:8], refs[8]
    step = pl.program_id(0)
    if again:
        left, _, out, quarter, band = refs[9:]
    else:
        upper, panel, out, quarter, left, band = refs[9:]

        @pl.when(step == 0)
        def _():
            left_of(info, panel, upper, left)

    half = info[8] if again else info[7]
    width = band.shape[1]
    columns = pl.ds(pl.multiple_of(half * 512 + step * width, width), width)
    place_rows(band, own, other, info, columns)
    keep = lax.broadcasted_iota(jnp.int32, (SN, width), 0)
    r = [split(jnp.where(keep < info[4 + s], band[SN * s:SN * s + SN, :], 0.0)) for s in range(NSN)]
    s0 = split(dot3(lower[0], r[0]))
    s1 = split(dot3(lower[1], r[0]) + dot3(lower[2], r[1]))
    s2 = split(dot3(lower[3], r[0]) + dot3(lower[4], r[1]) + dot3(lower[5], r[2]))
    order = order_of(info, info[2] * 1024 + half * 512 + step * width, 1, (1, width))
    total = None
    for s, value in enumerate((s0, s1, s2)):
        live = order > s
        masked = tuple(jnp.where(live, part, jnp.zeros_like(part)) for part in value)
        term = dot3(left[:, SN * s:SN * s + SN], masked)
        total = term if total is None else total + term
    for i in range(4):
        rows = slice(128 * i, 128 * i + 128)
        result = front[rows, :] * kept[i:i + 1, columns] - total[rows]
        out[rows, :] = result
        if i % 2:
            for j in range(width // 256):
                quarter[64 * (i - 1):64 * (i + 1), 128 * j:128 * j + 128] = result[:, 256 * j + 128:256 * j + 256]


VMEM_WHOLE = pl.BlockSpec(memory_space=pltpu.VMEM)


def each(axis_size, target):
    return [(i, target(i)) for i in range(axis_size)]


X_UP = each(ROWS, lambda i: (i + 4) % ROWS)
X_DOWN = each(ROWS, lambda i: (i - 4) % ROWS)
MATE = each(ROWS, lambda i: i ^ 2)
CORE = each(ROWS, lambda i: i ^ 1)
Z_ODD = [(z, z + 1) for z in range(0, COLS, 2)]


def gather_plane(piece, odd):
    height = piece.shape[0]
    mate = lax.ppermute(piece, "row", MATE)
    pair = jnp.concatenate([jnp.where(odd, mate, piece), jnp.where(odd, piece, mate)])
    before = lax.ppermute(pair, "row", X_UP)
    after = lax.ppermute(pair, "row", X_DOWN)
    far_even = lax.ppermute(before[:height], "row", X_UP)
    far_odd = lax.ppermute(after[height:], "row", X_DOWN)
    own = [pair, after, jnp.concatenate([far_even, far_odd]), before]
    return own, [lax.ppermute(part, "row", CORE) for part in own]


def exchange(front, kept, info, row_index, col_index):
    odd = (row_index // 2) % 2 == 1
    odd_col = col_index % 2 == 1
    moved = lax.ppermute(front[384:512] * kept[3:4], "row", [(0, 1)])
    pieces = pl.pallas_call(
        pieces_kernel,
        grid_spec=pltpu.PrefetchScalarGridSpec(
            num_scalar_prefetch=1,
            grid=(),
            in_specs=[VMEM_WHOLE] * 3,
            out_specs=[VMEM_WHOLE] * CHIPS,
        ),
        out_shape=[jax.ShapeDtypeStruct((48, 1024), jnp.float32)] * CHIPS,
        name="pieces",
    )(info, front, kept, moved)
    parts = [lax.ppermute(pieces[q], "row", [(0, 2 * q), (1, 2 * q + 1)]) for q in range(1, CHIPS)]
    piece = jnp.where(row_index < 2, pieces[0], sum(parts[1:], parts[0]))

    core_piece = piece[:, :PIV]
    parts = [lax.ppermute(core_piece, "col", [(0, z)]) for z in (2, 4, 6)]
    pivot_piece = jnp.where(col_index == 0, core_piece, parts[0] + parts[1] + parts[2])
    pivot_piece = jnp.where(odd_col, lax.ppermute(pivot_piece, "col", Z_ODD), pivot_piece)

    strips = [front[64 * z:64 * z + 64, :PIV] * kept[z // 2:z // 2 + 1, :PIV] for z in range(COLS)]
    parts = [lax.ppermute(strips[z], "col", [(0, z)]) for z in range(1, COLS)]
    strip = jnp.where(col_index == 0, strips[0], sum(parts[1:], parts[0]))
    panel = lax.all_to_all(jnp.broadcast_to(strip[None], (COLS, 64, PIV)), "col", 0, 0).reshape(512, PIV)

    return gather_plane(piece, odd), gather_plane(pivot_piece, odd), panel


def compute(info, front, kept, band, pivot, panel):
    stacked = lambda *n: jax.ShapeDtypeStruct((*n, 2 * SN, SN), jnp.bfloat16)
    lower, upper = pl.pallas_call(
        factor_kernel,
        grid_spec=pltpu.PrefetchScalarGridSpec(
            num_scalar_prefetch=1,
            grid=(),
            in_specs=[VMEM_WHOLE] * 8,
            out_specs=[VMEM_WHOLE] * 2,
            scratch_shapes=[pltpu.VMEM((PIV, PIV), jnp.float32)],
        ),
        out_shape=[stacked(6), stacked(3)],
        name="factor",
    )(info, *pivot[0], *pivot[1])
    width = 512

    def update(which, *inputs):
        def at(j, info):
            return (0, info[7 + which] * (512 // width) + j)

        left_shape = (1024, PIV)
        specs = [VMEM_WHOLE, pl.BlockSpec(memory_space=pl.ANY)] if which else [VMEM_WHOLE] * len(inputs)
        return pl.pallas_call(
            lambda *refs: update_kernel(*refs, again=which == 1),
            grid_spec=pltpu.PrefetchScalarGridSpec(
                num_scalar_prefetch=1,
                grid=(512 // width,),
                in_specs=[pl.BlockSpec((512, width), at)] + [VMEM_WHOLE] * 10 + specs,
                out_specs=[
                    pl.BlockSpec((512, width), at),
                    pl.BlockSpec((256, width // 2), lambda j, info: (0, j)),
                ] + [VMEM_WHOLE] * (1 - which),
                scratch_shapes=[pltpu.VMEM((PIV, width), jnp.float32)],
            ),
            out_shape=[
                jax.ShapeDtypeStruct((512, 1024), jnp.float32),
                jax.ShapeDtypeStruct((256, 256), jnp.float32),
            ] + [jax.ShapeDtypeStruct(left_shape, jnp.bfloat16)] * (1 - which),
            input_output_aliases={13: 0} if which else {},
            name="update",
        )(info, front, kept, *band[0], *band[1], lower, *inputs)

    partial, leaving, left = update(0, upper, panel)
    arriving = lax.ppermute(leaving, "depth", [(0, 1), (1, 0)])
    result, staying = update(1, left, partial)
    return result[None], staying + arriving


def local(front_matrix, block_mask, supernode_width):
    row_index = lax.axis_index("row")
    col_index = lax.axis_index("col")
    depth_index = lax.axis_index("depth")
    block_rows = row_index * 4 + jnp.arange(4)
    block_cols = col_index * 8 + jnp.arange(8)
    kept = ((block_mask[0] != 0) | (block_rows[:, None] == block_cols[None, :])).astype(jnp.float32)
    kept = jnp.broadcast_to(kept[:, :, None], (4, 8, BLK)).reshape(4, 1024)
    front = front_matrix[0]
    info = jnp.concatenate([
        jnp.stack([row_index // 4, row_index % 2, col_index, row_index]).astype(jnp.int32),
        supernode_width[0],
        jnp.stack([1 - depth_index, depth_index]).astype(jnp.int32),
    ])
    panels = exchange(front, kept, info, row_index, col_index)
    return compute(info, front, kept, *panels)


def solution(mesh):
    placed = (P("depth", "row", "col"), P("depth", "row", "col"), P("depth", None))
    return jax.shard_map(
        local,
        mesh=mesh,
        in_specs=placed,
        out_specs=(P("depth", "row", "col"), P("row", ("col", "depth"))),
        check_vma=False,
    )
```
